1024 devices in a mesh: tensor: 16 (over y, x_hi, core), context: 64 (over x_lo, z).
Axes of the slice: x: 4 (x_hi: 2, x_lo: 2; x = x_hi * 2 + x_lo), y: 4, z: 32, core: 2. Of those that a mesh axis runs over, the one named last changes fastest.
Arguments:
- query: float32 [8192, 8192], P('context', 'tensor'), may hold values from -6 to 6
- keys: float32 [8192, 8192], P('context', 'tensor'), may hold values from -6 to 6
- values: float32 [8192, 8192], P('context', 'tensor'), may hold values from -6 to 6
- filters: float32 [8192, 512], P('context', 'tensor'), may hold values from -0.0625 to 0.0625
- w_out: bfloat16 [8192, 8192], P('tensor'), may hold values from -0.09375 to 0.09375
- grad_z: float32 [8192, 8192], P('context', 'tensor'), may hold values from -0.015625 to 0.015625
Outputs:
- out: float32 [8192, 8192], P('context', 'tensor')
- grad_filters: float32 [8192, 512], P('context', 'tensor')
The draws below stay inside these ranges and needn't reach their ends.
All inputs are finite; a program needn't handle non-finite values.
Results may differ from the reference program's by a relative error of at most 0.009.
Values sent between devices are 32-bit elements; how exact they have to be, the bound alone decides.
No kernel may reach another device: no remote copies, remote signals or barrier semaphores. Data moves between devices by JAX's collectives and lax.ppermute only.
A program may use at most 64 MiB of HBM per device.

```python
import jax
import jax.numpy as jnp
from jax import lax

D = 8192
FGROUP = 16
SEQ = 8192
FILTERS = 512


def strengthened(drawn, own_key, source, target, blocks, factor):
    def block_of(axis_at):
        return (jnp.arange(drawn.shape[axis_at]) // (drawn.shape[axis_at] // blocks)).reshape((-1,) + (1,) * (drawn.ndim - 1 - axis_at))

    one_side = jax.random.permutation(own_key, blocks)[block_of(target)]
    other_side = (block_of(target) + blocks // 2) % blocks
    return jnp.where((block_of(source) == one_side) | (block_of(source) == other_side), factor * drawn, drawn)


def shard_levels(own_key, shape, pieces, smallest, high):
    gain = 1.0
    for position, shards_of in pieces:
        steps = jax.random.uniform(jax.random.fold_in(jax.random.fold_in(own_key, 6), position), (shards_of,), jnp.float32, smallest / len(pieces), high / len(pieces))
        gain = gain * jnp.repeat(jnp.exp(steps), shape[position] // shards_of).reshape((-1,) + (1,) * (len(shape) - 1 - position))
    return gain


def scatter_about(key, dims, deviation, reach, shards=(), kind=jnp.bfloat16):
    entries = deviation * jax.random.normal(key, dims, jnp.float32)
    if shards:
        entries = entries * shard_levels(key, dims, shards, -0.22, 0.18)
    return jnp.clip(entries, -reach, reach).astype(kind)


def gaussian_with(key, extent, scale, most, split, heavy, kind=jnp.bfloat16):
    array = scale * jax.random.normal(key, extent, jnp.float32)
    if split:
        array = array * shard_levels(key, extent, split, -0.22, 0.18)
    return jnp.clip(strengthened(array, jax.random.fold_in(key, 3), *heavy), -most, most).astype(kind)


def setup_inputs(seed: int = 0) -> dict:
    seeds = jax.random.split(jax.random.key(seed), 7)
    query = scatter_about(seeds[0], (SEQ, D), 1.0, 6.0, ((0, 64), (1, 16)), jnp.float32)
    keys = scatter_about(seeds[1], (SEQ, D), 1.0, 6.0, ((0, 64), (1, 16)), jnp.float32)
    values = scatter_about(seeds[2], (SEQ, D), 1.0, 6.0, ((0, 64), (1, 16)), jnp.float32)
    filters = scatter_about(seeds[3], (SEQ, FILTERS), SEQ ** -0.5, 0.0625, ((0, 64), (1, 16)), jnp.float32)
    w_out = gaussian_with(seeds[4], (D, D), D ** -0.5, 0.09375, ((0, 16),), (0, 1, 16, 2.0))
    grad_z = scatter_about(seeds[5], (SEQ, D), (FGROUP * SEQ) ** -0.5, 0.015625, ((0, 64), (1, 16)), jnp.float32)
    return dict(query=query, keys=keys, values=values, filters=filters, w_out=w_out, grad_z=grad_z)


def reference(query, keys, values, filters, w_out, grad_z):
    length = query.shape[0]
    padded = 2 * length
    width = FGROUP * 8
    blocks = D // width

    def one_block(index):
        start = (index * width).astype(jnp.int32)
        fstart = (index * 8).astype(jnp.int32)
        query_blk = lax.dynamic_slice_in_dim(query, start, width, 1)
        keys_blk = lax.dynamic_slice_in_dim(keys, start, width, 1)
        values_blk = lax.dynamic_slice_in_dim(values, start, width, 1)
        grad_blk = lax.dynamic_slice_in_dim(grad_z, start, width, 1)
        filt_blk = lax.dynamic_slice_in_dim(filters, fstart, 8, 1)
        gated = keys_blk * values_blk
        backin = grad_blk * query_blk
        gated_spec = jnp.fft.rfft(gated, n=padded, axis=0)
        back_spec = jnp.fft.rfft(backin, n=padded, axis=0)
        filt_spec = jnp.fft.rfft(filt_blk, n=padded, axis=0)
        wide_filt = jnp.repeat(filt_spec, FGROUP, axis=1)
        conv = jnp.fft.irfft(wide_filt * gated_spec, n=padded, axis=0)[:length]
        cross = back_spec * jnp.conj(gated_spec)
        cross = cross.reshape(cross.shape[0], 8, FGROUP).sum(axis=2)
        grad_blk_filt = jnp.fft.irfft(cross, n=padded, axis=0)[:length]
        mixed = query_blk * conv
        return mixed, grad_blk_filt

    mixed_all, grad_all = lax.map(one_block, jnp.arange(blocks, dtype=jnp.int32))
    mixed = jnp.transpose(mixed_all, (1, 0, 2)).reshape(length, D).astype(jnp.float32)
    grad_filters = jnp.transpose(grad_all, (1, 0, 2)).reshape(length, D // FGROUP).astype(jnp.float32)
    mixed_half = mixed.astype(jnp.bfloat16)
    out = jnp.dot(mixed_half, w_out, preferred_element_type=jnp.float32)
    return out, grad_filters
```

```python
import jax
import jax.numpy as jnp
import numpy as np
from jax import lax
from jax.experimental import pallas as pl
from jax.experimental.pallas import tpu as pltpu
from jax.sharding import Mesh, PartitionSpec as P

FINE = (("y", 4), ("xh", 2), ("core", 2), ("xl", 2), ("z", 32))
TENSOR = ("y", "xh", "core")
CONTEXT = ("xl", "z")
ROWS = 8
B = 128
F32 = jnp.float32
BF16 = jnp.bfloat16
VMEM = pl.BlockSpec(memory_space=pltpu.VMEM)


def gate_kernel(q_ref, k_ref, v_ref, f_ref, z_ref, out_ref):
    n = out_ref.shape[0]
    gated = (k_ref[...] * v_ref[...]).T
    backin = (z_ref[...] * q_ref[...]).T
    filt = f_ref[...]
    out_ref[:, 0:ROWS, :] = gated.reshape(n, ROWS, B)
    out_ref[:, ROWS : 2 * ROWS, :] = backin.reshape(n, ROWS, B)
    share = n // filt.shape[0]
    for j in range(n):
        out_ref[j, 2 * ROWS : 2 * ROWS + 1, :] = filt[j // share : j // share + 1, :]


def gate(q, k, v, f, z, parts):
    return pl.pallas_call(
        gate_kernel,
        out_shape=jax.ShapeDtypeStruct((parts, 2 * ROWS + 1, B), F32),
        in_specs=[VMEM] * 5,
        out_specs=VMEM,
        name="gate",
    )(q, k, v, f.T, z)


def wide(x):
    x = x.reshape(x.shape[0] // 2, 2, ROWS, B)
    return jnp.concatenate([x[:, 0], x[:, 1]], axis=-1).reshape(-1, 2 * B)


def conv_kernel(in_ref, out_ref, filt_ref, toep_ref, pad_ref, flip_ref, acc_ref, outer_ref, pos_ref, neg_ref):
    nb = in_ref.shape[0]
    half = nb // 2
    rows = half * ROWS
    row = lax.broadcasted_iota(jnp.int32, (B, B), 0)
    lane = lax.broadcasted_iota(jnp.int32, (B, B), 1)
    for j in range(nb):
        filt_ref[j : j + 1, :] = in_ref[j, 2 * ROWS : 2 * ROWS + 1, :]
    toep_ref[nb * B : (nb + 1) * B, :] = jnp.zeros((B, B), BF16)

    def build(dist, before):
        taps = jnp.broadcast_to(filt_ref[pl.ds(dist, 1), :], (B, B))
        now = pltpu.roll(taps, 0, 1, stride=1, stride_axis=0)
        at = pl.multiple_of((nb - 1 - dist) * B, B)
        toep_ref[pl.ds(at, B), :] = jnp.where(lane >= row, now, before).astype(BF16)
        return now

    lax.fori_loop(0, nb, build, jnp.zeros((B, B), F32), unroll=4)

    pad_ref[0:rows, :] = jnp.zeros((rows, 2 * B), F32)
    gated = wide(in_ref[:, 0:ROWS, :])
    pad_ref[rows : 2 * rows, :] = gated
    flip = jnp.where(lane + row == B - 1, 1.0, 0.0).astype(BF16)
    flip_ref[0:rows, :] = jnp.zeros((rows, 2 * B), F32)
    for p in range(2):
        part = gated[:, p * B : (p + 1) * B].astype(BF16)
        flip_ref[rows : 2 * rows, p * B : (p + 1) * B] = jnp.dot(part, flip, preferred_element_type=F32)
    back_t = wide(in_ref[:, ROWS : 2 * ROWS, :]).T.astype(BF16)
    acc_ref[...] = jnp.zeros((rows, 2 * B), F32)

    def step(d, carried):
        start = pl.multiple_of(rows - ROWS * d, ROWS)
        shifted = pad_ref[pl.ds(start, rows), :].astype(BF16)
        even = pl.multiple_of((nb - 1 - 2 * d) * B, B)
        odd = pl.multiple_of((nb - 2 - 2 * d) * B, B)
        taps = jnp.concatenate([toep_ref[pl.ds(even, 2 * B), :], toep_ref[pl.ds(odd, 2 * B), :]], axis=1)
        acc_ref[...] += jnp.dot(shifted, taps, preferred_element_type=F32)
        flipped = flip_ref[pl.ds(start, rows), :].astype(BF16)
        outer = jnp.dot(back_t, flipped, preferred_element_type=F32)
        outer_ref[2 * d] = carried + outer[0:B, B : 2 * B]
        outer_ref[2 * d + 1] = outer[0:B, 0:B] + outer[B : 2 * B, B : 2 * B]
        return outer[B : 2 * B, 0:B]

    outer_ref[nb] = lax.fori_loop(0, half, step, jnp.zeros((B, B), F32), unroll=2)

    later = (lane < row) | (lane == B - 1)

    def diagonals(dist, _):
        rolled = pltpu.roll(outer_ref[dist + 1], 0, 1, stride=1, stride_axis=0)
        kept = jnp.where(later, rolled, 0.0)
        pos_ref[pl.ds(dist, 1), :] = jnp.sum(kept, axis=0, keepdims=True)
        neg_ref[pl.ds(dist, 1), :] = jnp.sum(rolled - kept, axis=0, keepdims=True)
        return 0

    lax.fori_loop(0, nb, diagonals, 0, unroll=4)
    neg_ref[nb : nb + 1, :] = jnp.zeros((1, B), F32)
    turned = pos_ref[...] + neg_ref[1 : nb + 1, :]
    pos_ref[...] = pltpu.roll(turned, 1, 1)
    for p in range(2):
        out_ref[:, p, 0:ROWS, :] = acc_ref[:, p * B : (p + 1) * B].reshape(half, ROWS, B)
    for j in range(nb):
        out_ref[j // 2, j % 2, ROWS : ROWS + 1, :] = pos_ref[j : j + 1, :]


def convolve(x):
    nb = x.shape[0]
    half = nb // 2
    y = pl.pallas_call(
        conv_kernel,
        out_shape=jax.ShapeDtypeStruct((half, 2, ROWS + 1, B), F32),
        in_specs=[VMEM],
        out_specs=VMEM,
        scratch_shapes=[
            pltpu.VMEM((nb, B), F32),
            pltpu.VMEM(((nb + 1) * B, B), BF16),
            pltpu.VMEM((2 * half * ROWS, 2 * B), F32),
            pltpu.VMEM((2 * half * ROWS, 2 * B), F32),
            pltpu.VMEM((half * ROWS, 2 * B), F32),
            pltpu.VMEM((nb + 1, B, B), F32),
            pltpu.VMEM((nb, B), F32),
            pltpu.VMEM((nb + 8, B), F32),
        ],
        name="conv",
    )(x)
    return y.reshape(nb, ROWS + 1, B)


def first_kernel(core_ref, q_ref, c_ref, w_ref, out_ref, mixed_ref):
    @pl.when(pl.program_id(0) == 0)
    def _():
        conv = c_ref[:, 0:ROWS, :].reshape(-1, B).T
        mixed_ref[...] = (q_ref[...] * conv).astype(BF16)

    out_ref[0] = jnp.dot(mixed_ref[...], w_ref[...], preferred_element_type=F32)


def second_kernel(core_ref, mixed_ref, w_ref, out_ref):
    out_ref[0] = jnp.dot(mixed_ref[...], w_ref[...], preferred_element_type=F32)


def project(q, c, w, core, n):
    slab, chans = q.shape
    wide_n = w.shape[1] // n
    pairs = n // 2
    cost = pl.CostEstimate(flops=slab * chans * w.shape[1], bytes_accessed=w.size, transcendentals=0)
    out = jax.ShapeDtypeStruct((pairs, slab, wide_n), F32)
    out_spec = pl.BlockSpec((1, slab, wide_n), lambda i, s: (i, 0, 0))
    w_spec = pl.BlockSpec((chans, wide_n), lambda i, s: (0, 2 * i + s[0]))

    def fixed(shape):
        return pl.BlockSpec(shape, lambda i, s: (0,) * len(shape))

    theirs, mixed = pl.pallas_call(
        first_kernel,
        out_shape=(out, jax.ShapeDtypeStruct((slab, chans), BF16)),
        grid_spec=pltpu.PrefetchScalarGridSpec(
            num_scalar_prefetch=1,
            grid=(pairs,),
            in_specs=[fixed(q.shape), fixed(c.shape), w_spec],
            out_specs=(out_spec, fixed((slab, chans))),
        ),
        cost_estimate=cost,
        name="theirs",
    )((1 - core).reshape(1), q, c, w)
    mine = pl.pallas_call(
        second_kernel,
        out_shape=out,
        grid_spec=pltpu.PrefetchScalarGridSpec(
            num_scalar_prefetch=1,
            grid=(pairs,),
            in_specs=[fixed((slab, chans)), w_spec],
            out_specs=out_spec,
        ),
        cost_estimate=cost,
        name="mine",
    )(core.reshape(1), mixed, w)
    return theirs, mine


def on_device(query, keys, values, filters, w_out, grad_z):
    parts = lax.axis_size(CONTEXT)
    n = lax.axis_size(TENSOR)
    nfilt = filters.shape[1]
    core = lax.axis_index("core").astype(jnp.int32)
    sent = gate(query, keys, values, filters, grad_z, parts)
    whole = lax.all_to_all(sent, CONTEXT, split_axis=0, concat_axis=0, tiled=True)
    result = convolve(whole)
    back = lax.all_to_all(result, CONTEXT, split_axis=0, concat_axis=0, tiled=True)
    theirs, mine = project(query, back, w_out, core, n)
    swapped = lax.ppermute(theirs, "core", [(0, 1), (1, 0)])
    grad_filters = back[:, ROWS, :].reshape(nfilt, parts // nfilt, B).sum(axis=1).T
    summed = mine + swapped
    pieces = lax.all_to_all(summed, ("y", "xh"), split_axis=0, concat_axis=0, tiled=True)
    return jnp.sum(pieces, axis=0), grad_filters


def solution(mesh):
    fine = Mesh(
        np.asarray(mesh.devices).reshape([size for _, size in FINE]),
        [name for name, _ in FINE],
    )
    both = P(CONTEXT, TENSOR)
    return jax.shard_map(
        on_device,
        mesh=fine,
        in_specs=(both, both, both, both, P(TENSOR, None), both),
        out_specs=(both, both),
        check_vma=False,
    )
```

```python
import jax
import jax.numpy as jnp
import numpy as np
from jax import lax
from jax.experimental import pallas as pl
from jax.experimental.pallas import tpu as pltpu
from jax.sharding import Mesh, PartitionSpec as P

FINE = (("y", 4), ("xh", 2), ("core", 2), ("xl", 2), ("z", 32))
TENSOR = ("y", "xh", "core")
CONTEXT = ("xl", "z")
ROWS = 8
B = 128
F32 = jnp.float32
BF16 = jnp.bfloat16
VMEM = pl.BlockSpec(memory_space=pltpu.VMEM)
HBM = pl.BlockSpec(memory_space=pltpu.HBM)


def params(mib):
    return pltpu.CompilerParams(vmem_limit_bytes=mib << 20)


def gate_kernel(q_hbm, k_hbm, v_hbm, z_hbm, f_hbm, out_ref, in_ref, f_ref, turn_ref, sem):
    width = 2 * ROWS + 1
    n = out_ref.shape[0] // width
    share = n // f_ref.shape[0]
    copies = [pltpu.make_async_copy(f_hbm, f_ref, sem.at[4])]
    for i, hbm in enumerate((k_hbm, v_hbm, z_hbm, q_hbm)):
        copies.append(pltpu.make_async_copy(hbm, in_ref.at[i], sem.at[i]))
    for copy in copies:
        copy.start()
    copies[0].wait()
    for r in range(share):
        out_ref[pl.ds(r * width + 2 * ROWS, n // share, stride=share * width), :] = f_ref[...]
    for i in range(2):
        copies[2 * i + 1].wait()
        copies[2 * i + 2].wait()
        turn_ref[i] = (in_ref[2 * i] * in_ref[2 * i + 1]).T
        for r in range(ROWS):
            rows = turn_ref[i, pl.ds(r, n, stride=ROWS), :]
            out_ref[pl.ds(i * ROWS + r, n, stride=width), :] = rows


def gate(q, k, v, f, z, parts):
    return pl.pallas_call(
        gate_kernel,
        out_shape=jax.ShapeDtypeStruct((parts * (2 * ROWS + 1), B), F32),
        in_specs=[HBM] * 5,
        out_specs=VMEM,
        scratch_shapes=[
            pltpu.VMEM((4,) + q.shape, F32),
            pltpu.VMEM(f.shape[::-1], F32),
            pltpu.VMEM((2, q.shape[1], B), F32),
            pltpu.SemaphoreType.DMA((5,)),
        ],
        compiler_params=params(60),
        name="gate",
    )(q, k, v, z, f.T)


def beside(x):
    return jnp.concatenate([x[0], x[1]], axis=-1)


def conv_kernel(in_ref, out_ref, filt_ref, toep_ref, pad_ref, flip_ref, acc_ref, outer_ref, pos_ref, neg_ref):
    width = 2 * ROWS + 1
    nb = in_ref.shape[0] // width
    half = nb // 2
    rows = half * ROWS
    row = lax.broadcasted_iota(jnp.int32, (B, B), 0)
    lane = lax.broadcasted_iota(jnp.int32, (B, B), 1)
    filt_ref[...] = in_ref[pl.ds(2 * ROWS, nb, stride=width), :]
    toep_ref[nb * B : (nb + 1) * B, :] = jnp.zeros((B, B), BF16)

    def build(dist, before):
        taps = jnp.broadcast_to(filt_ref[pl.ds(dist, 1), :], (B, B))
        now = pltpu.roll(taps, 0, 1, stride=1, stride_axis=0)
        at = pl.multiple_of((nb - 1 - dist) * B, B)
        toep_ref[pl.ds(at, B), :] = jnp.where(lane >= row, now, before).astype(BF16)
        return now

    lax.fori_loop(0, nb, build, jnp.zeros((B, B), F32), unroll=4)

    for r in range(ROWS):
        for p in range(2):
            take = in_ref[pl.ds(r + p * width, half, stride=2 * width), :]
            pad_ref[p, pl.ds(rows + r, half, stride=ROWS), :] = take
            take = in_ref[pl.ds(ROWS + r + p * width, half, stride=2 * width), :]
            acc_ref[p, pl.ds(r, half, stride=ROWS), :] = take
    pad_ref[:, 0:rows, :] = jnp.zeros((2, rows, B), F32)
    flip = jnp.where(lane + row == B - 1, 1.0, 0.0).astype(BF16)
    flip_ref[:, 0:rows, :] = jnp.zeros((2, rows, B), F32)
    for p in range(2):
        part = pad_ref[p, rows : 2 * rows, :].astype(BF16)
        flip_ref[p, rows : 2 * rows, :] = jnp.dot(part, flip, preferred_element_type=F32)
    back_t = beside(acc_ref[...]).T.astype(BF16)
    acc_ref[...] = jnp.zeros((2, rows, B), F32)

    def step(d, carried):
        start = pl.multiple_of(rows - ROWS * d, ROWS)
        shifted = beside(pad_ref[:, pl.ds(start, rows), :]).astype(BF16)
        even = pl.multiple_of((nb - 1 - 2 * d) * B, B)
        odd = pl.multiple_of((nb - 2 - 2 * d) * B, B)
        taps = jnp.concatenate([toep_ref[pl.ds(even, 2 * B), :], toep_ref[pl.ds(odd, 2 * B), :]], axis=1)
        ahead = jnp.dot(shifted, taps, preferred_element_type=F32)
        acc_ref[0] += ahead[:, 0:B]
        acc_ref[1] += ahead[:, B : 2 * B]
        flipped = beside(flip_ref[:, pl.ds(start, rows), :]).astype(BF16)
        outer = jnp.dot(back_t, flipped, preferred_element_type=F32)
        outer_ref[2 * d] = carried + outer[0:B, B : 2 * B]
        outer_ref[2 * d + 1] = outer[0:B, 0:B] + outer[B : 2 * B, B : 2 * B]
        return outer[B : 2 * B, 0:B]

    outer_ref[nb] = lax.fori_loop(0, half, step, jnp.zeros((B, B), F32), unroll=2)

    later = (lane < row) | (lane == B - 1)

    def diagonals(dist, _):
        rolled = pltpu.roll(outer_ref[dist + 1], 0, 1, stride=1, stride_axis=0)
        kept = jnp.where(later, rolled, 0.0)
        pos_ref[pl.ds(dist, 1), :] = jnp.sum(kept, axis=0, keepdims=True)
        neg_ref[pl.ds(dist, 1), :] = jnp.sum(rolled - kept, axis=0, keepdims=True)
        return 0

    lax.fori_loop(0, nb, diagonals, 0, unroll=4)
    neg_ref[nb : nb + 1, :] = jnp.zeros((1, B), F32)
    turned = pos_ref[...] + neg_ref[1 : nb + 1, :]
    pos_ref[...] = pltpu.roll(turned, 1, 1)
    for r in range(ROWS):
        for p in range(2):
            at = pl.ds(r + p * (ROWS + 1), half, stride=2 * (ROWS + 1))
            out_ref[at, :] = acc_ref[p, pl.ds(r, half, stride=ROWS), :]
    out_ref[pl.ds(ROWS, nb, stride=ROWS + 1), :] = pos_ref[...]


def convolve(x):
    nb = x.shape[0] // (2 * ROWS + 1)
    half = nb // 2
    return pl.pallas_call(
        conv_kernel,
        out_shape=jax.ShapeDtypeStruct((nb * (ROWS + 1), B), F32),
        in_specs=[VMEM],
        out_specs=VMEM,
        scratch_shapes=[
            pltpu.VMEM((nb, B), F32),
            pltpu.VMEM(((nb + 1) * B, B), BF16),
            pltpu.VMEM((2, 2 * half * ROWS, B), F32),
            pltpu.VMEM((2, 2 * half * ROWS, B), F32),
            pltpu.VMEM((2, half * ROWS, B), F32),
            pltpu.VMEM((nb + 1, B, B), F32),
            pltpu.VMEM((nb, B), F32),
            pltpu.VMEM((nb + 8, B), F32),
        ],
        compiler_params=params(16),
        name="conv",
    )(x)


def fetch(core_ref, w_hbm, w_ref, sem):
    pairs, _, wide_n = w_ref.shape

    def copy(i):
        at = pl.multiple_of((2 * i + core_ref[0]) * wide_n, wide_n)
        return pltpu.make_async_copy(w_hbm.at[:, pl.ds(at, wide_n)], w_ref.at[i], sem.at[i])

    for i in range(pairs):
        copy(i).start()
    return lambda i: copy(i).wait()


def multiply(mixed_ref, w_ref, out_ref, wait):
    def block(i, _):
        wait(i)
        out_ref[i] = jnp.dot(mixed_ref[...], w_ref[i], preferred_element_type=F32)
        return 0

    lax.fori_loop(0, w_ref.shape[0], block, 0)


def first_kernel(core_ref, q_hbm, c_ref, w_hbm, out_ref, mixed_ref, df_ref, q_ref, turn_ref, w_ref, q_sem, w_sem):
    width = ROWS + 1
    n = c_ref.shape[0] // width
    nfilt = df_ref.shape[0]
    q_copy = pltpu.make_async_copy(q_hbm, q_ref, q_sem)
    q_copy.start()
    wait = fetch(core_ref, w_hbm, w_ref, w_sem)
    for r in range(ROWS):
        turn_ref[pl.ds(r, n, stride=ROWS), :] = c_ref[pl.ds(r, n, stride=width), :]
    share = n // nfilt
    total = c_ref[pl.ds(ROWS, nfilt, stride=share * width), :]
    for r in range(1, share):
        total += c_ref[pl.ds(r * width + ROWS, nfilt, stride=share * width), :]
    df_ref[...] = total
    q_copy.wait()
    mixed_ref[...] = (q_ref[...] * turn_ref[...].T).astype(BF16)
    multiply(mixed_ref, w_ref, out_ref, wait)


def second_kernel(core_ref, mixed_ref, w_hbm, out_ref, w_ref, w_sem):
    multiply(mixed_ref, w_ref, out_ref, fetch(core_ref, w_hbm, w_ref, w_sem))


def project(q, c, w, core, n, nfilt):
    slab, chans = q.shape
    wide_n = w.shape[1] // n
    pairs = n // 2
    cost = pl.CostEstimate(flops=slab * chans * w.shape[1], bytes_accessed=w.size, transcendentals=0)
    out = jax.ShapeDtypeStruct((pairs, slab, wide_n), F32)
    mix = jax.ShapeDtypeStruct((slab, chans), BF16)
    df = jax.ShapeDtypeStruct((nfilt, B), F32)
    smem = pl.BlockSpec(memory_space=pltpu.SMEM)
    weights = [pltpu.VMEM((pairs, chans, wide_n), BF16)]
    sems = [pltpu.SemaphoreType.DMA((pairs,))]
    theirs, mixed, df = pl.pallas_call(
        first_kernel,
        out_shape=(out, mix, df),
        in_specs=[smem, HBM, VMEM, HBM],
        out_specs=(VMEM, VMEM, VMEM),
        scratch_shapes=[
            pltpu.VMEM(q.shape, F32),
            pltpu.VMEM((chans, B), F32),
            *weights,
            pltpu.SemaphoreType.DMA(()),
            *sems,
        ],
        cost_estimate=cost,
        compiler_params=params(46),
        name="theirs",
    )((1 - core).reshape(1), q, c, w)
    mine = pl.pallas_call(
        second_kernel,
        out_shape=out,
        in_specs=[smem, VMEM, HBM],
        out_specs=VMEM,
        scratch_shapes=weights + sems,
        cost_estimate=cost,
        compiler_params=params(46),
        name="mine",
    )(core.reshape(1), mixed, w)
    return theirs, mine, df


def on_device(query, keys, values, filters, w_out, grad_z):
    parts = lax.axis_size(CONTEXT)
    n = lax.axis_size(TENSOR)
    nfilt = filters.shape[1]
    core = lax.axis_index("core").astype(jnp.int32)

    def exchange(x):
        x = x.reshape(parts, 1, -1)
        return lax.all_to_all(x, CONTEXT, split_axis=0, concat_axis=0, tiled=True).reshape(-1, B)

    whole = exchange(gate(query, keys, values, filters, grad_z, parts))
    back = exchange(convolve(whole))
    theirs, mine, grad_filters = project(query, back, w_out, core, n, nfilt)
    swapped = lax.ppermute(theirs, "core", [(0, 1), (1, 0)])
    summed = mine + swapped
    pieces = lax.all_to_all(summed, ("y", "xh"), split_axis=0, concat_axis=0, tiled=True)
    return jnp.sum(pieces, axis=0), grad_filters.T


def solution(mesh):
    fine = Mesh(
        np.asarray(mesh.devices).reshape([size for _, size in FINE]),
        [name for name, _ in FINE],
    )
    both = P(CONTEXT, TENSOR)
    return jax.shard_map(
        on_device,
        mesh=fine,
        in_specs=(both, both, both, both, P(TENSOR, None), both),
        out_specs=(both, both),
        check_vma=False,
    )
```

```python
import jax
import jax.numpy as jnp
import numpy as np
from jax import lax
from jax.experimental import pallas as pl
from jax.experimental.pallas import tpu as pltpu
from jax.sharding import Mesh, PartitionSpec as P

FINE = (("y", 4), ("xh", 2), ("core", 2), ("xl", 2), ("z", 32))
TENSOR = ("y", "xh", "core")
CONTEXT = ("xl", "z")
ROWS = 8
B = 128
F32 = jnp.float32
BF16 = jnp.bfloat16
VMEM = pl.BlockSpec(memory_space=pltpu.VMEM)
HBM = pl.BlockSpec(memory_space=pltpu.HBM)


def params(mib):
    return pltpu.CompilerParams(vmem_limit_bytes=mib << 20)


def gate_kernel(q_hbm, k_hbm, v_hbm, z_hbm, f_hbm, out_ref, in_ref, f_ref, turn_ref, sem):
    width = 2 * ROWS + 1
    n = out_ref.shape[0] // width
    share = n // f_ref.shape[0]
    copies = [pltpu.make_async_copy(f_hbm, f_ref, sem.at[4])]
    for i, hbm in enumerate((k_hbm, v_hbm, z_hbm, q_hbm)):
        copies.append(pltpu.make_async_copy(hbm, in_ref.at[i], sem.at[i]))
    for copy in copies:
        copy.start()
    copies[0].wait()
    for r in range(share):
        out_ref[pl.ds(r * width + 2 * ROWS, n // share, stride=share * width), :] = f_ref[...]
    for i in range(2):
        copies[2 * i + 1].wait()
        copies[2 * i + 2].wait()
        turn_ref[i] = (in_ref[2 * i] * in_ref[2 * i + 1]).T
        for r in range(ROWS):
            rows = turn_ref[i, pl.ds(r, n, stride=ROWS), :]
            out_ref[pl.ds(i * ROWS + r, n, stride=width), :] = rows


def gate(q, k, v, f, z, parts):
    return pl.pallas_call(
        gate_kernel,
        out_shape=jax.ShapeDtypeStruct((parts * (2 * ROWS + 1), B), F32),
        in_specs=[HBM] * 5,
        out_specs=VMEM,
        scratch_shapes=[
            pltpu.VMEM((4,) + q.shape, F32),
            pltpu.VMEM(f.shape[::-1], F32),
            pltpu.VMEM((2, q.shape[1], B), F32),
            pltpu.SemaphoreType.DMA((5,)),
        ],
        compiler_params=params(60),
        name="gate",
    )(q, k, v, z, f.T)


def beside(x):
    return jnp.concatenate([x[0], x[1]], axis=-1)


def conv_kernel(in_ref, out_ref, filt_ref, toep_ref, pad_ref, flip_ref, back_ref, acc_ref, outer_ref, diag_ref):
    width = 2 * ROWS + 1
    nb = in_ref.shape[0] // width
    half = nb // 2
    rows = half * ROWS
    row = lax.broadcasted_iota(jnp.int32, (B, B), 0)
    lane = lax.broadcasted_iota(jnp.int32, (B, B), 1)
    filt_ref[0:1, :] = jnp.zeros((1, B), F32)
    filt_ref[nb + 1 :, :] = jnp.zeros((7, B), F32)
    filt_ref[pl.ds(1, nb), :] = in_ref[pl.ds(2 * ROWS, nb, stride=width), :]
    for r in range(ROWS):
        for p in range(2):
            take = in_ref[pl.ds(r + p * width, half, stride=2 * width), :]
            pad_ref[p, pl.ds(rows + r, half, stride=ROWS), :] = take
            take = in_ref[pl.ds(ROWS + r + p * width, half, stride=2 * width), :]
            acc_ref[p, pl.ds(r, half, stride=ROWS), :] = take
    pad_ref[:, 0:rows, :] = jnp.zeros((2, rows, B), F32)
    flip = jnp.where(lane + row == B - 1, 1.0, 0.0).astype(BF16)
    flip_ref[:, 0:rows, :] = jnp.zeros((2, rows, B), F32)
    for p in range(2):
        part = pad_ref[p, rows : 2 * rows, :].astype(BF16)
        flip_ref[p, rows : 2 * rows, :] = jnp.dot(part, flip, preferred_element_type=F32)
    back_ref[...] = beside(acc_ref[...]).T.astype(BF16)
    acc_ref[...] = jnp.zeros((2, rows, B), F32)
    outer_ref[0:4] = jnp.zeros((4, B, B), F32)

    toep_ref[(nb + 2) * B :, :] = jnp.zeros((B, B), BF16)

    def build(dist):
        now = jnp.broadcast_to(filt_ref[pl.ds(dist + 1, 1), :], (B, B))
        before = jnp.broadcast_to(filt_ref[pl.ds(dist, 1), :], (B, B))
        block = pltpu.roll(jnp.where(lane + row < B, now, before), 0, 1, stride=1, stride_axis=0)
        at = pl.multiple_of((nb + 1 - dist) * B, B)
        toep_ref[pl.ds(at, B), :] = block.astype(BF16)

    def diagonal(at):
        picked = jnp.where(lane + row >= B - 1, outer_ref[at], outer_ref[at + 1])
        rolled = pltpu.roll(picked, 0, 1, stride=1, stride_axis=0)
        diag_ref[pl.ds(at, 1), :] = jnp.sum(rolled, axis=0, keepdims=True)

    def step(d, live, deep):
        even = pl.multiple_of((nb + 1 - 2 * d) * B, B)
        odd = pl.multiple_of((nb - 2 * d) * B, B)
        taps = jnp.concatenate([toep_ref[pl.ds(even, 2 * B), :], toep_ref[pl.ds(odd, 2 * B), :]], axis=1)
        start = pl.multiple_of(2 * rows - live - ROWS * d, ROWS)
        shifted = beside(pad_ref[:, pl.ds(start, live), :]).astype(BF16)
        ahead = jnp.dot(shifted, taps, preferred_element_type=F32)
        start = pl.multiple_of(2 * rows - deep - ROWS * d, ROWS)
        flipped = beside(flip_ref[:, pl.ds(start, deep), :]).astype(BF16)
        outer = jnp.dot(back_ref[:, rows - deep :], flipped, preferred_element_type=F32)
        build(2 * d + 2)
        build(2 * d + 3)
        diagonal(2 * d)
        diagonal(2 * d + 1)
        acc_ref[0, rows - live :, :] += ahead[:, 0:B]
        acc_ref[1, rows - live :, :] += ahead[:, B : 2 * B]
        outer_ref[2 * d + 3] += outer[0:B, B : 2 * B]
        outer_ref[2 * d + 4] = outer[0:B, 0:B] + outer[B : 2 * B, B : 2 * B]
        outer_ref[2 * d + 5] = outer[B : 2 * B, 0:B]

    build(0)
    build(1)
    phases = 4
    for phase in range(phases):
        live = rows * (phases - phase) // phases
        deep = min(rows, -(-live // B) * B)

        def some(d, _, live=live, deep=deep):
            step(d, live, deep)
            return 0

        lax.fori_loop(half * phase // phases, half * (phase + 1) // phases, some, 0, unroll=8)
    outer_ref[nb + 4] = jnp.zeros((B, B), F32)
    for at in range(nb, nb + 4):
        diagonal(at)
    for r in range(ROWS):
        for p in range(2):
            at = pl.ds(r + p * (ROWS + 1), half, stride=2 * (ROWS + 1))
            out_ref[at, :] = acc_ref[p, pl.ds(r, half, stride=ROWS), :]
    out_ref[pl.ds(ROWS, nb, stride=ROWS + 1), :] = pltpu.roll(diag_ref[pl.ds(4, nb), :], 1, 1)


def convolve(x):
    nb = x.shape[0] // (2 * ROWS + 1)
    half = nb // 2
    return pl.pallas_call(
        conv_kernel,
        out_shape=jax.ShapeDtypeStruct((nb * (ROWS + 1), B), F32),
        in_specs=[VMEM],
        out_specs=VMEM,
        scratch_shapes=[
            pltpu.VMEM((nb + 8, B), F32),
            pltpu.VMEM(((nb + 3) * B, B), BF16),
            pltpu.VMEM((2, 2 * half * ROWS, B), F32),
            pltpu.VMEM((2, 2 * half * ROWS, B), F32),
            pltpu.VMEM((2 * B, half * ROWS), BF16),
            pltpu.VMEM((2, half * ROWS, B), F32),
            pltpu.VMEM((nb + 6, B, B), F32),
            pltpu.VMEM((nb + 8, B), F32),
        ],
        compiler_params=params(16),
        name="conv",
    )(x)


def fetch(core_ref, w_hbm, w_ref, sem):
    pairs, _, wide_n = w_ref.shape

    def copy(i):
        at = pl.multiple_of((2 * i + core_ref[0]) * wide_n, wide_n)
        return pltpu.make_async_copy(w_hbm.at[:, pl.ds(at, wide_n)], w_ref.at[i], sem.at[i])

    for i in range(pairs):
        copy(i).start()
    return lambda i: copy(i).wait()


def multiply(mixed_ref, w_ref, out_ref, wait):
    def block(i, _):
        wait(i)
        out_ref[i] = jnp.dot(mixed_ref[...], w_ref[i], preferred_element_type=F32)
        return 0

    lax.fori_loop(0, w_ref.shape[0], block, 0)


def first_kernel(core_ref, q_hbm, c_ref, w_hbm, out_ref, mixed_ref, df_ref, q_ref, turn_ref, w_ref, q_sem, w_sem):
    width = ROWS + 1
    n = c_ref.shape[0] // width
    nfilt = df_ref.shape[0]
    q_copy = pltpu.make_async_copy(q_hbm, q_ref, q_sem)
    q_copy.start()
    wait = fetch(core_ref, w_hbm, w_ref, w_sem)
    for r in range(ROWS):
        turn_ref[pl.ds(r, n, stride=ROWS), :] = c_ref[pl.ds(r, n, stride=width), :]
    share = n // nfilt
    total = c_ref[pl.ds(ROWS, nfilt, stride=share * width), :]
    for r in range(1, share):
        total += c_ref[pl.ds(r * width + ROWS, nfilt, stride=share * width), :]
    df_ref[...] = total
    q_copy.wait()
    mixed_ref[...] = (q_ref[...] * turn_ref[...].T).astype(BF16)
    multiply(mixed_ref, w_ref, out_ref, wait)


def second_kernel(core_ref, mixed_ref, w_hbm, out_ref, w_ref, w_sem):
    multiply(mixed_ref, w_ref, out_ref, fetch(core_ref, w_hbm, w_ref, w_sem))


def project(q, c, w, core, n, nfilt):
    slab, chans = q.shape
    wide_n = w.shape[1] // n
    pairs = n // 2
    cost = pl.CostEstimate(flops=slab * chans * w.shape[1], bytes_accessed=w.size, transcendentals=0)
    out = jax.ShapeDtypeStruct((pairs, slab, wide_n), F32)
    mix = jax.ShapeDtypeStruct((slab, chans), BF16)
    df = jax.ShapeDtypeStruct((nfilt, B), F32)
    smem = pl.BlockSpec(memory_space=pltpu.SMEM)
    weights = [pltpu.VMEM((pairs, chans, wide_n), BF16)]
    sems = [pltpu.SemaphoreType.DMA((pairs,))]
    theirs, mixed, df = pl.pallas_call(
        first_kernel,
        out_shape=(out, mix, df),
        in_specs=[smem, HBM, VMEM, HBM],
        out_specs=(VMEM, VMEM, VMEM),
        scratch_shapes=[
            pltpu.VMEM(q.shape, F32),
            pltpu.VMEM((chans, B), F32),
            *weights,
            pltpu.SemaphoreType.DMA(()),
            *sems,
        ],
        cost_estimate=cost,
        compiler_params=params(46),
        name="theirs",
    )((1 - core).reshape(1), q, c, w)
    mine = pl.pallas_call(
        second_kernel,
        out_shape=out,
        in_specs=[smem, VMEM, HBM],
        out_specs=VMEM,
        scratch_shapes=weights + sems,
        cost_estimate=cost,
        compiler_params=params(46),
        name="mine",
    )(core.reshape(1), mixed, w)
    return theirs, mine, df


def on_device(query, keys, values, filters, w_out, grad_z):
    parts = lax.axis_size(CONTEXT)
    n = lax.axis_size(TENSOR)
    nfilt = filters.shape[1]
    core = lax.axis_index("core").astype(jnp.int32)

    def exchange(x):
        x = x.reshape(parts, 1, -1)
        return lax.all_to_all(x, CONTEXT, split_axis=0, concat_axis=0, tiled=True).reshape(-1, B)

    whole = exchange(gate(query, keys, values, filters, grad_z, parts))
    back = exchange(convolve(whole))
    theirs, mine, grad_filters = project(query, back, w_out, core, n, nfilt)
    swapped = lax.ppermute(theirs, "core", [(0, 1), (1, 0)])
    summed = mine + swapped
    pieces = lax.all_to_all(summed, ("y", "xh"), split_axis=0, concat_axis=0, tiled=True)
    return jnp.sum(pieces, axis=0), grad_filters.T


def solution(mesh):
    fine = Mesh(
        np.asarray(mesh.devices).reshape([size for _, size in FINE]),
        [name for name, _ in FINE],
    )
    both = P(CONTEXT, TENSOR)
    return jax.shard_map(
        on_device,
        mesh=fine,
        in_specs=(both, both, both, both, P(TENSOR, None), both),
        out_specs=(both, both),
        check_vma=False,
    )
```

```python
import jax
import jax.numpy as jnp
import numpy as np
from jax import lax
from jax.experimental import pallas as pl
from jax.experimental.pallas import tpu as pltpu
from jax.sharding import Mesh, PartitionSpec as P

FINE = (("y", 4), ("xh", 2), ("core", 2), ("xl", 2), ("z", 32))
TENSOR = ("y", "xh", "core")
CONTEXT = ("xl", "z")
ROWS = 8
B = 128
F32 = jnp.float32
BF16 = jnp.bfloat16
VMEM = pl.BlockSpec(memory_space=pltpu.VMEM)
HBM = pl.BlockSpec(memory_space=pltpu.HBM)


def params(mib):
    return pltpu.CompilerParams(vmem_limit_bytes=mib << 20)


def gate_kernel(q_hbm, k_hbm, v_hbm, z_hbm, f_hbm, out_hbm, in_ref, f_ref, turn_ref, out_ref, sem, f_sem, out_sem):
    width = 2 * ROWS + 1
    groups = out_sem.shape[0]
    n = out_ref.shape[0] // width // groups
    share = n * groups // f_ref.shape[0]
    pairs = ((k_hbm, v_hbm), (z_hbm, q_hbm))

    def fetch(g, i, j):
        at = pl.ds(g * B, B)
        return pltpu.make_async_copy(pairs[i][j].at[:, at], in_ref.at[2 * i + j, :, at], sem.at[g, 2 * i + j])

    def send(g):
        at = pl.ds(g * n * width, n * width)
        return pltpu.make_async_copy(out_ref.at[at], out_hbm.at[at], out_sem.at[g])

    f_copy = pltpu.make_async_copy(f_hbm, f_ref, f_sem)
    for g in range(groups):
        for i in range(2):
            for j in range(2):
                fetch(g, i, j).start()
        if g == 0:
            f_copy.start()
    f_copy.wait()
    for r in range(share):
        at = pl.ds(r * width + 2 * ROWS, f_ref.shape[0], stride=share * width)
        out_ref[at, :] = f_ref[...]
    for g in range(groups):
        for i in range(2):
            fetch(g, i, 0).wait()
            fetch(g, i, 1).wait()
            at = pl.ds(g * B, B)
            turn_ref[i, at, :] = (in_ref[2 * i, :, at] * in_ref[2 * i + 1, :, at]).T
            for r in range(ROWS):
                rows = turn_ref[i, pl.ds(g * B + r, n, stride=ROWS), :]
                out_ref[pl.ds(g * n * width + i * ROWS + r, n, stride=width), :] = rows
        send(g).start()
    for g in range(groups):
        send(g).wait()


def gate(q, k, v, f, z, parts):
    return pl.pallas_call(
        gate_kernel,
        out_shape=jax.ShapeDtypeStruct((parts * (2 * ROWS + 1), B), F32),
        in_specs=[HBM] * 5,
        out_specs=HBM,
        scratch_shapes=[
            pltpu.VMEM((4,) + q.shape, F32),
            pltpu.VMEM(f.shape[::-1], F32),
            pltpu.VMEM((2, q.shape[1], B), F32),
            pltpu.VMEM((parts * (2 * ROWS + 1), B), F32),
            pltpu.SemaphoreType.DMA((q.shape[1] // B, 4)),
            pltpu.SemaphoreType.DMA(()),
            pltpu.SemaphoreType.DMA((q.shape[1] // B,)),
        ],
        compiler_params=params(60),
        name="gate",
    )(q, k, v, z, f.T)


def beside(x):
    return jnp.concatenate([x[0], x[1]], axis=-1)


def conv_kernel(in_ref, out_ref, filt_ref, toep_ref, pad_ref, flip_ref, back_ref, acc_ref, outer_ref, diag_ref):
    width = 2 * ROWS + 1
    nb = in_ref.shape[0] // width
    half = nb // 2
    rows = half * ROWS
    row = lax.broadcasted_iota(jnp.int32, (B, B), 0)
    lane = lax.broadcasted_iota(jnp.int32, (B, B), 1)
    filt_ref[0:1, :] = jnp.zeros((1, B), F32)
    filt_ref[nb + 1 :, :] = jnp.zeros((7, B), F32)
    filt_ref[pl.ds(1, nb), :] = in_ref[pl.ds(2 * ROWS, nb, stride=width), :]
    for r in range(ROWS):
        for p in range(2):
            take = in_ref[pl.ds(r + p * width, half, stride=2 * width), :]
            pad_ref[p, pl.ds(rows + r, half, stride=ROWS), :] = take
            take = in_ref[pl.ds(ROWS + r + p * width, half, stride=2 * width), :]
            acc_ref[p, pl.ds(r, half, stride=ROWS), :] = take
    pad_ref[:, 0:rows, :] = jnp.zeros((2, rows, B), F32)
    flip = jnp.where(lane + row == B - 1, 1.0, 0.0).astype(BF16)
    flip_ref[:, 0:rows, :] = jnp.zeros((2, rows, B), F32)
    for p in range(2):
        part = pad_ref[p, rows : 2 * rows, :].astype(BF16)
        flip_ref[p, rows : 2 * rows, :] = jnp.dot(part, flip, preferred_element_type=F32)
    back_ref[...] = beside(acc_ref[...]).T.astype(BF16)
    acc_ref[...] = jnp.zeros((2, rows, B), F32)
    outer_ref[0:4] = jnp.zeros((4, B, B), F32)

    toep_ref[(nb + 2) * B :, :] = jnp.zeros((B, B), BF16)

    def build(dist):
        now = jnp.broadcast_to(filt_ref[pl.ds(dist + 1, 1), :], (B, B))
        before = jnp.broadcast_to(filt_ref[pl.ds(dist, 1), :], (B, B))
        block = pltpu.roll(jnp.where(lane + row < B, now, before), 0, 1, stride=1, stride_axis=0)
        at = pl.multiple_of((nb + 1 - dist) * B, B)
        toep_ref[pl.ds(at, B), :] = block.astype(BF16)

    def diagonal(at):
        picked = jnp.where(lane + row >= B - 1, outer_ref[at], outer_ref[at + 1])
        rolled = pltpu.roll(picked, 0, 1, stride=1, stride_axis=0)
        diag_ref[pl.ds(at, 1), :] = jnp.sum(rolled, axis=0, keepdims=True)

    def step(d, live, deep):
        even = pl.multiple_of((nb + 1 - 2 * d) * B, B)
        odd = pl.multiple_of((nb - 2 * d) * B, B)
        taps = jnp.concatenate([toep_ref[pl.ds(even, 2 * B), :], toep_ref[pl.ds(odd, 2 * B), :]], axis=1)
        start = pl.multiple_of(2 * rows - live - ROWS * d, ROWS)
        shifted = beside(pad_ref[:, pl.ds(start, live), :]).astype(BF16)
        ahead = jnp.dot(shifted, taps, preferred_element_type=F32)
        start = pl.multiple_of(2 * rows - deep - ROWS * d, ROWS)
        flipped = beside(flip_ref[:, pl.ds(start, deep), :]).astype(BF16)
        outer = jnp.dot(back_ref[:, rows - deep :], flipped, preferred_element_type=F32)
        build(2 * d + 2)
        build(2 * d + 3)
        diagonal(2 * d)
        diagonal(2 * d + 1)
        acc_ref[0, rows - live :, :] += ahead[:, 0:B]
        acc_ref[1, rows - live :, :] += ahead[:, B : 2 * B]
        outer_ref[2 * d + 3] += outer[0:B, B : 2 * B]
        outer_ref[2 * d + 4] = outer[0:B, 0:B] + outer[B : 2 * B, B : 2 * B]
        outer_ref[2 * d + 5] = outer[B : 2 * B, 0:B]

    build(0)
    build(1)
    phases = 4
    for phase in range(phases):
        live = rows * (phases - phase) // phases
        deep = min(rows, -(-live // B) * B)

        def some(d, _, live=live, deep=deep):
            step(d, live, deep)
            return 0

        lax.fori_loop(half * phase // phases, half * (phase + 1) // phases, some, 0, unroll=8)
    outer_ref[nb + 4] = jnp.zeros((B, B), F32)
    for at in range(nb, nb + 4):
        diagonal(at)
    for r in range(ROWS):
        for p in range(2):
            at = pl.ds(r + p * (ROWS + 1), half, stride=2 * (ROWS + 1))
            out_ref[at, :] = acc_ref[p, pl.ds(r, half, stride=ROWS), :]
    out_ref[pl.ds(ROWS, nb, stride=ROWS + 1), :] = pltpu.roll(diag_ref[pl.ds(4, nb), :], 1, 1)


def convolve(x):
    nb = x.shape[0] // (2 * ROWS + 1)
    half = nb // 2
    return pl.pallas_call(
        conv_kernel,
        out_shape=jax.ShapeDtypeStruct((nb * (ROWS + 1), B), F32),
        in_specs=[VMEM],
        out_specs=VMEM,
        scratch_shapes=[
            pltpu.VMEM((nb + 8, B), F32),
            pltpu.VMEM(((nb + 3) * B, B), BF16),
            pltpu.VMEM((2, 2 * half * ROWS, B), F32),
            pltpu.VMEM((2, 2 * half * ROWS, B), F32),
            pltpu.VMEM((2 * B, half * ROWS), BF16),
            pltpu.VMEM((2, half * ROWS, B), F32),
            pltpu.VMEM((nb + 6, B, B), F32),
            pltpu.VMEM((nb + 8, B), F32),
        ],
        compiler_params=params(16),
        name="conv",
    )(x)


def fetch(core_ref, w_hbm, w_ref, sem, first):
    blocks, _, wide_n = w_ref.shape

    def copy(i):
        at = pl.multiple_of((2 * (first + i) + core_ref[0]) * wide_n, wide_n)
        return pltpu.make_async_copy(w_hbm.at[:, pl.ds(at, wide_n)], w_ref.at[i], sem.at[i])

    for i in range(blocks):
        copy(i).start()
    return lambda i: copy(i).wait()


def fetch_kernel(core_ref, after_ref, w_hbm, out_ref, sem):
    wait = fetch(core_ref, w_hbm, out_ref, sem, 0)
    for i in range(out_ref.shape[0]):
        wait(i)


def multiply(mixed_ref, w_ref, out_ref, first):
    for i in range(w_ref.shape[0]):
        out_ref[first + i] = jnp.dot(mixed_ref[...], w_ref[i], preferred_element_type=F32)


def first_kernel(core_ref, q_ref, c_ref, ahead_ref, w_hbm, out_ref, mixed_ref, df_ref, turn_ref, w_ref, w_sem):
    width = ROWS + 1
    n = c_ref.shape[0] // width
    nfilt = df_ref.shape[0]
    early = ahead_ref.shape[0]
    wait = fetch(core_ref, w_hbm, w_ref, w_sem, early)
    for r in range(ROWS):
        turn_ref[pl.ds(r, n, stride=ROWS), :] = c_ref[pl.ds(r, n, stride=width), :]
    mixed_ref[...] = (q_ref[...] * turn_ref[...].T).astype(BF16)
    share = n // nfilt
    total = c_ref[pl.ds(ROWS, nfilt, stride=share * width), :]
    for r in range(1, share):
        total += c_ref[pl.ds(r * width + ROWS, nfilt, stride=share * width), :]
    df_ref[...] = total
    multiply(mixed_ref, ahead_ref, out_ref, 0)
    for i in range(w_ref.shape[0]):
        wait(i)
    multiply(mixed_ref, w_ref, out_ref, early)


def second_kernel(core_ref, mixed_ref, w_hbm, out_ref, w_ref, w_sem):
    wait = fetch(core_ref, w_hbm, w_ref, w_sem, 0)
    half = w_ref.shape[0] // 2
    for start in (0, half):
        for i in range(half):
            wait(start + i)
        multiply(mixed_ref, w_ref.at[start : start + half], out_ref, start)


SMEM = pl.BlockSpec(memory_space=pltpu.SMEM)


def prefetch(after, w, core, n):
    shape = (n // 4, w.shape[0], w.shape[1] // n)
    return pl.pallas_call(
        fetch_kernel,
        out_shape=jax.ShapeDtypeStruct(shape, BF16),
        in_specs=[SMEM, pl.BlockSpec(memory_space=pl.ANY), HBM],
        out_specs=VMEM,
        scratch_shapes=[pltpu.SemaphoreType.DMA(shape[:1])],
        cost_estimate=pl.CostEstimate(flops=0, bytes_accessed=w.size, transcendentals=0),
        compiler_params=params(46),
        name="prefetch",
    )((1 - core).reshape(1), after, w)


def project(q, c, w, w_theirs, core, nfilt):
    slab, chans = q.shape
    early, _, wide_n = w_theirs.shape
    pairs = w.shape[1] // wide_n // 2
    cost = pl.CostEstimate(flops=slab * chans * w.shape[1], bytes_accessed=w.size, transcendentals=0)
    out = jax.ShapeDtypeStruct((pairs, slab, wide_n), F32)
    mix = jax.ShapeDtypeStruct((slab, chans), BF16)
    df = jax.ShapeDtypeStruct((nfilt, B), F32)
    theirs, mixed, df = pl.pallas_call(
        first_kernel,
        out_shape=(out, mix, df),
        in_specs=[SMEM, VMEM, VMEM, VMEM, HBM],
        out_specs=(VMEM, VMEM, VMEM),
        scratch_shapes=[
            pltpu.VMEM((chans, B), F32),
            pltpu.VMEM((pairs - early, chans, wide_n), BF16),
            pltpu.SemaphoreType.DMA((pairs - early,)),
        ],
        cost_estimate=cost,
        compiler_params=params(46),
        name="theirs",
    )((1 - core).reshape(1), q, c, w_theirs, w)
    mine = pl.pallas_call(
        second_kernel,
        out_shape=out,
        in_specs=[SMEM, VMEM, HBM],
        out_specs=VMEM,
        scratch_shapes=[pltpu.VMEM((pairs, chans, wide_n), BF16), pltpu.SemaphoreType.DMA((pairs,))],
        cost_estimate=cost,
        compiler_params=params(46),
        name="mine",
    )(core.reshape(1), mixed, w)
    return theirs, mine, df


def on_device(query, keys, values, filters, w_out, grad_z):
    parts = lax.axis_size(CONTEXT)
    n = lax.axis_size(TENSOR)
    nfilt = filters.shape[1]
    core = lax.axis_index("core").astype(jnp.int32)

    def exchange(x):
        x = x.reshape(parts, 1, -1)
        return lax.all_to_all(x, CONTEXT, split_axis=0, concat_axis=0, tiled=True).reshape(-1, B)

    whole = exchange(gate(query, keys, values, filters, grad_z, parts))
    result = convolve(whole)
    w_theirs = prefetch(result, w_out, core, n)
    back = exchange(result)
    theirs, mine, grad_filters = project(query, back, w_out, w_theirs, core, nfilt)
    swapped = lax.ppermute(theirs, "core", [(0, 1), (1, 0)])
    summed = mine + swapped
    pieces = lax.all_to_all(summed, ("y", "xh"), split_axis=0, concat_axis=0, tiled=True)
    return jnp.sum(pieces, axis=0), grad_filters.T


def solution(mesh):
    fine = Mesh(
        np.asarray(mesh.devices).reshape([size for _, size in FINE]),
        [name for name, _ in FINE],
    )
    both = P(CONTEXT, TENSOR)
    return jax.shard_map(
        on_device,
        mesh=fine,
        in_specs=(both, both, both, both, P(TENSOR, None), both),
        out_specs=(both, both),
        check_vma=False,
    )
```

```python
import jax
import jax.numpy as jnp
import numpy as np
from jax import lax
from jax.experimental import pallas as pl
from jax.experimental.pallas import tpu as pltpu
from jax.sharding import Mesh, PartitionSpec as P

FINE = (("y", 4), ("xh", 2), ("core", 2), ("xl", 2), ("z", 32))
TENSOR = ("y", "xh", "core")
CONTEXT = ("xl", "z")
ROWS = 8
B = 128
F32 = jnp.float32
BF16 = jnp.bfloat16
VMEM = pl.BlockSpec(memory_space=pltpu.VMEM)
HBM = pl.BlockSpec(memory_space=pltpu.HBM)
SMEM = pl.BlockSpec(memory_space=pltpu.SMEM)
LATER_NS = 12000


def params(mib):
    return pltpu.CompilerParams(vmem_limit_bytes=mib << 20)


def gate_kernel(wait_ref, q_hbm, k_hbm, v_hbm, z_hbm, f_hbm, out_ref, in_ref, f_ref, turn_ref, sem):
    width = 2 * ROWS + 1
    n = out_ref.shape[0] // width
    share = n // f_ref.shape[0]
    copies = [pltpu.make_async_copy(f_hbm, f_ref, sem.at[4])]
    for i, hbm in enumerate((k_hbm, v_hbm, z_hbm, q_hbm)):
        copies.append(pltpu.make_async_copy(hbm, in_ref.at[i], sem.at[i]))
    for copy in copies:
        copy.start()
    copies[0].wait()
    for r in range(share):
        out_ref[pl.ds(r * width + 2 * ROWS, n // share, stride=share * width), :] = f_ref[...]
    for i in range(2):
        copies[2 * i + 1].wait()
        copies[2 * i + 2].wait()
        turn_ref[i] = (in_ref[2 * i] * in_ref[2 * i + 1]).T
        for r in range(ROWS):
            rows = turn_ref[i, pl.ds(r, n, stride=ROWS), :]
            out_ref[pl.ds(i * ROWS + r, n, stride=width), :] = rows

    @pl.when(wait_ref[0] == 1)
    def _():
        pl.delay(LATER_NS)


def gate(q, k, v, f, z, parts, later):
    return pl.pallas_call(
        gate_kernel,
        out_shape=jax.ShapeDtypeStruct((parts * (2 * ROWS + 1), B), F32),
        in_specs=[SMEM] + [HBM] * 5,
        out_specs=VMEM,
        scratch_shapes=[
            pltpu.VMEM((4,) + q.shape, F32),
            pltpu.VMEM(f.shape[::-1], F32),
            pltpu.VMEM((2, q.shape[1], B), F32),
            pltpu.SemaphoreType.DMA((5,)),
        ],
        compiler_params=params(60),
        name="gate",
    )(later.reshape(1), q, k, v, z, f.T)


def beside(x):
    return jnp.concatenate([x[0], x[1]], axis=-1)


def conv_kernel(in_ref, out_ref, filt_ref, toep_ref, pad_ref, flip_ref, back_ref, acc_ref, outer_ref, diag_ref):
    width = 2 * ROWS + 1
    nb = in_ref.shape[0] // width
    half = nb // 2
    rows = half * ROWS
    row = lax.broadcasted_iota(jnp.int32, (B, B), 0)
    lane = lax.broadcasted_iota(jnp.int32, (B, B), 1)
    filt_ref[0:1, :] = jnp.zeros((1, B), F32)
    filt_ref[nb + 1 :, :] = jnp.zeros((7, B), F32)
    filt_ref[pl.ds(1, nb), :] = in_ref[pl.ds(2 * ROWS, nb, stride=width), :]
    for r in range(ROWS):
        for p in range(2):
            take = in_ref[pl.ds(r + p * width, half, stride=2 * width), :]
            pad_ref[p, pl.ds(rows + r, half, stride=ROWS), :] = take
            take = in_ref[pl.ds(ROWS + r + p * width, half, stride=2 * width), :]
            acc_ref[p, pl.ds(r, half, stride=ROWS), :] = take
    pad_ref[:, 0:rows, :] = jnp.zeros((2, rows, B), F32)
    flip = jnp.where(lane + row == B - 1, 1.0, 0.0).astype(BF16)
    flip_ref[:, 0:rows, :] = jnp.zeros((2, rows, B), F32)
    for p in range(2):
        part = pad_ref[p, rows : 2 * rows, :].astype(BF16)
        flip_ref[p, rows : 2 * rows, :] = jnp.dot(part, flip, preferred_element_type=F32)
    back_ref[...] = beside(acc_ref[...]).T.astype(BF16)
    acc_ref[...] = jnp.zeros((2, rows, B), F32)
    outer_ref[0:4] = jnp.zeros((4, B, B), F32)

    toep_ref[(nb + 2) * B :, :] = jnp.zeros((B, B), BF16)

    def build(dist):
        now = jnp.broadcast_to(filt_ref[pl.ds(dist + 1, 1), :], (B, B))
        before = jnp.broadcast_to(filt_ref[pl.ds(dist, 1), :], (B, B))
        block = pltpu.roll(jnp.where(lane + row < B, now, before), 0, 1, stride=1, stride_axis=0)
        at = pl.multiple_of((nb + 1 - dist) * B, B)
        toep_ref[pl.ds(at, B), :] = block.astype(BF16)

    def diagonal(at):
        picked = jnp.where(lane + row >= B - 1, outer_ref[at], outer_ref[at + 1])
        rolled = pltpu.roll(picked, 0, 1, stride=1, stride_axis=0)
        diag_ref[pl.ds(at, 1), :] = jnp.sum(rolled, axis=0, keepdims=True)

    def step(d, live, deep):
        even = pl.multiple_of((nb + 1 - 2 * d) * B, B)
        odd = pl.multiple_of((nb - 2 * d) * B, B)
        taps = jnp.concatenate([toep_ref[pl.ds(even, 2 * B), :], toep_ref[pl.ds(odd, 2 * B), :]], axis=1)
        start = pl.multiple_of(2 * rows - live - ROWS * d, ROWS)
        shifted = beside(pad_ref[:, pl.ds(start, live), :]).astype(BF16)
        ahead = jnp.dot(shifted, taps, preferred_element_type=F32)
        start = pl.multiple_of(2 * rows - deep - ROWS * d, ROWS)
        flipped = beside(flip_ref[:, pl.ds(start, deep), :]).astype(BF16)
        outer = jnp.dot(back_ref[:, rows - deep :], flipped, preferred_element_type=F32)
        build(2 * d + 2)
        build(2 * d + 3)
        diagonal(2 * d)
        diagonal(2 * d + 1)
        acc_ref[0, rows - live :, :] += ahead[:, 0:B]
        acc_ref[1, rows - live :, :] += ahead[:, B : 2 * B]
        outer_ref[2 * d + 3] += outer[0:B, B : 2 * B]
        outer_ref[2 * d + 4] = outer[0:B, 0:B] + outer[B : 2 * B, B : 2 * B]
        outer_ref[2 * d + 5] = outer[B : 2 * B, 0:B]

    build(0)
    build(1)
    phases = 4
    for phase in range(phases):
        live = rows * (phases - phase) // phases
        deep = min(rows, -(-live // B) * B)

        def some(d, _, live=live, deep=deep):
            step(d, live, deep)
            return 0

        lax.fori_loop(half * phase // phases, half * (phase + 1) // phases, some, 0, unroll=8)
    outer_ref[nb + 4] = jnp.zeros((B, B), F32)
    for at in range(nb, nb + 4):
        diagonal(at)
    for r in range(ROWS):
        for p in range(2):
            at = pl.ds(r + p * (ROWS + 1), half, stride=2 * (ROWS + 1))
            out_ref[at, :] = acc_ref[p, pl.ds(r, half, stride=ROWS), :]
    out_ref[pl.ds(ROWS, nb, stride=ROWS + 1), :] = pltpu.roll(diag_ref[pl.ds(4, nb), :], 1, 1)


def convolve(x):
    nb = x.shape[0] // (2 * ROWS + 1)
    half = nb // 2
    return pl.pallas_call(
        conv_kernel,
        out_shape=jax.ShapeDtypeStruct((nb * (ROWS + 1), B), F32),
        in_specs=[VMEM],
        out_specs=VMEM,
        scratch_shapes=[
            pltpu.VMEM((nb + 8, B), F32),
            pltpu.VMEM(((nb + 3) * B, B), BF16),
            pltpu.VMEM((2, 2 * half * ROWS, B), F32),
            pltpu.VMEM((2, 2 * half * ROWS, B), F32),
            pltpu.VMEM((2 * B, half * ROWS), BF16),
            pltpu.VMEM((2, half * ROWS, B), F32),
            pltpu.VMEM((nb + 6, B, B), F32),
            pltpu.VMEM((nb + 8, B), F32),
        ],
        compiler_params=params(16),
        name="conv",
    )(x)


def fetch(core_ref, w_hbm, w_ref, sem, first):
    blocks, _, wide_n = w_ref.shape

    def copy(i):
        at = pl.multiple_of((2 * (first + i) + core_ref[0]) * wide_n, wide_n)
        return pltpu.make_async_copy(w_hbm.at[:, pl.ds(at, wide_n)], w_ref.at[i], sem.at[i])

    for i in range(blocks):
        copy(i).start()
    return lambda i: copy(i).wait()


def fetch_kernel(core_ref, after_ref, w_hbm, out_ref, sem):
    wait = fetch(core_ref, w_hbm, out_ref, sem, 0)
    for i in range(out_ref.shape[0]):
        wait(i)


def multiply(mixed_ref, w_ref, out_ref, first):
    for i in range(w_ref.shape[0]):
        out_ref[first + i] = jnp.dot(mixed_ref[...], w_ref[i], preferred_element_type=F32)


def first_kernel(core_ref, q_ref, c_ref, ahead_ref, w_hbm, out_ref, mixed_ref, df_ref, turn_ref, w_ref, w_sem):
    width = ROWS + 1
    n = c_ref.shape[0] // width
    nfilt = df_ref.shape[0]
    early = ahead_ref.shape[0]
    wait = fetch(core_ref, w_hbm, w_ref, w_sem, early)
    for r in range(ROWS):
        turn_ref[pl.ds(r, n, stride=ROWS), :] = c_ref[pl.ds(r, n, stride=width), :]
    mixed_ref[...] = (q_ref[...] * turn_ref[...].T).astype(BF16)
    share = n // nfilt
    total = c_ref[pl.ds(ROWS, nfilt, stride=share * width), :]
    for r in range(1, share):
        total += c_ref[pl.ds(r * width + ROWS, nfilt, stride=share * width), :]
    df_ref[...] = total
    multiply(mixed_ref, ahead_ref, out_ref, 0)
    for i in range(w_ref.shape[0]):
        wait(i)
    multiply(mixed_ref, w_ref, out_ref, early)


def second_kernel(core_ref, mixed_ref, w_hbm, out_ref, w_ref, w_sem):
    wait = fetch(core_ref, w_hbm, w_ref, w_sem, 0)
    half = w_ref.shape[0] // 2
    for start in (0, half):
        for i in range(half):
            wait(start + i)
        multiply(mixed_ref, w_ref.at[start : start + half], out_ref, start)


def prefetch(after, w, core, n):
    shape = (n // 4, w.shape[0], w.shape[1] // n)
    return pl.pallas_call(
        fetch_kernel,
        out_shape=jax.ShapeDtypeStruct(shape, BF16),
        in_specs=[SMEM, pl.BlockSpec(memory_space=pl.ANY), HBM],
        out_specs=VMEM,
        scratch_shapes=[pltpu.SemaphoreType.DMA(shape[:1])],
        cost_estimate=pl.CostEstimate(flops=0, bytes_accessed=w.size, transcendentals=0),
        compiler_params=params(46),
        name="prefetch",
    )((1 - core).reshape(1), after, w)


def project(q, c, w, w_theirs, core, nfilt):
    slab, chans = q.shape
    early, _, wide_n = w_theirs.shape
    pairs = w.shape[1] // wide_n // 2
    cost = pl.CostEstimate(flops=slab * chans * w.shape[1], bytes_accessed=w.size, transcendentals=0)
    out = jax.ShapeDtypeStruct((pairs, slab, wide_n), F32)
    mix = jax.ShapeDtypeStruct((slab, chans), BF16)
    df = jax.ShapeDtypeStruct((nfilt, B), F32)
    theirs, mixed, df = pl.pallas_call(
        first_kernel,
        out_shape=(out, mix, df),
        in_specs=[SMEM, VMEM, VMEM, VMEM, HBM],
        out_specs=(VMEM, VMEM, VMEM),
        scratch_shapes=[
            pltpu.VMEM((chans, B), F32),
            pltpu.VMEM((pairs - early, chans, wide_n), BF16),
            pltpu.SemaphoreType.DMA((pairs - early,)),
        ],
        cost_estimate=cost,
        compiler_params=params(46),
        name="theirs",
    )((1 - core).reshape(1), q, c, w_theirs, w)
    mine = pl.pallas_call(
        second_kernel,
        out_shape=out,
        in_specs=[SMEM, VMEM, HBM],
        out_specs=VMEM,
        scratch_shapes=[pltpu.VMEM((pairs, chans, wide_n), BF16), pltpu.SemaphoreType.DMA((pairs,))],
        cost_estimate=cost,
        compiler_params=params(46),
        name="mine",
    )(core.reshape(1), mixed, w)
    return theirs, mine, df


def on_device(query, keys, values, filters, w_out, grad_z):
    parts = lax.axis_size(CONTEXT)
    n = lax.axis_size(TENSOR)
    nfilt = filters.shape[1]
    core = lax.axis_index("core").astype(jnp.int32)

    def exchange(x):
        x = x.reshape(parts, 1, -1)
        return lax.all_to_all(x, CONTEXT, split_axis=0, concat_axis=0, tiled=True).reshape(-1, B)

    whole = exchange(gate(query, keys, values, filters, grad_z, parts, 1 - core))
    result = convolve(whole)
    w_theirs = prefetch(result, w_out, core, n)
    back = exchange(result)
    theirs, mine, grad_filters = project(query, back, w_out, w_theirs, core, nfilt)
    swapped = lax.ppermute(theirs, "core", [(0, 1), (1, 0)])
    summed = mine + swapped
    pieces = lax.all_to_all(summed, ("y", "xh"), split_axis=0, concat_axis=0, tiled=True)
    return jnp.sum(pieces, axis=0), grad_filters.T


def solution(mesh):
    fine = Mesh(
        np.asarray(mesh.devices).reshape([size for _, size in FINE]),
        [name for name, _ in FINE],
    )
    both = P(CONTEXT, TENSOR)
    return jax.shard_map(
        on_device,
        mesh=fine,
        in_specs=(both, both, both, both, P(TENSOR, None), both),
        out_specs=(both, both),
        check_vma=False,
    )
```

```python
import jax
import jax.numpy as jnp
import numpy as np
from jax import lax
from jax.experimental import pallas as pl
from jax.experimental.pallas import tpu as pltpu
from jax.sharding import Mesh, PartitionSpec as P

FINE = (("y", 4), ("xh", 2), ("core", 2), ("xl", 2), ("z", 32))
TENSOR = ("y", "xh", "core")
CONTEXT = ("xl", "z")
ROWS = 8
B = 128
F32 = jnp.float32
BF16 = jnp.bfloat16
VMEM = pl.BlockSpec(memory_space=pltpu.VMEM)
HBM = pl.BlockSpec(memory_space=pltpu.HBM)
SMEM = pl.BlockSpec(memory_space=pltpu.SMEM)
LATER_NS = 19000


def params(mib):
    return pltpu.CompilerParams(vmem_limit_bytes=mib << 20)


def gate_kernel(wait_ref, q_hbm, k_hbm, v_hbm, z_hbm, f_hbm, out_ref, in_ref, f_ref, turn_ref, sem):
    width = 2 * ROWS + 1
    n = out_ref.shape[0] // width
    share = n // f_ref.shape[0]
    copies = [pltpu.make_async_copy(f_hbm, f_ref, sem.at[4])]
    for i, hbm in enumerate((k_hbm, v_hbm, z_hbm, q_hbm)):
        copies.append(pltpu.make_async_copy(hbm, in_ref.at[i], sem.at[i]))
    for copy in copies:
        copy.start()
    copies[0].wait()
    for r in range(share):
        out_ref[pl.ds(r * width + 2 * ROWS, n // share, stride=share * width), :] = f_ref[...]
    for i in range(2):
        copies[2 * i + 1].wait()
        copies[2 * i + 2].wait()
        turn_ref[i] = (in_ref[2 * i] * in_ref[2 * i + 1]).T
        for r in range(ROWS):
            rows = turn_ref[i, pl.ds(r, n, stride=ROWS), :]
            out_ref[pl.ds(i * ROWS + r, n, stride=width), :] = rows

    @pl.when(wait_ref[0] == 1)
    def _():
        pl.delay(LATER_NS)


def gate(q, k, v, f, z, parts, later):
    return pl.pallas_call(
        gate_kernel,
        out_shape=jax.ShapeDtypeStruct((parts * (2 * ROWS + 1), B), F32),
        in_specs=[SMEM] + [HBM] * 5,
        out_specs=VMEM,
        scratch_shapes=[
            pltpu.VMEM((4,) + q.shape, F32),
            pltpu.VMEM(f.shape[::-1], F32),
            pltpu.VMEM((2, q.shape[1], B), F32),
            pltpu.SemaphoreType.DMA((5,)),
        ],
        compiler_params=params(60),
        name="gate",
    )(later.reshape(1), q, k, v, z, f.T)


def beside(x):
    return jnp.concatenate([x[0], x[1]], axis=-1)


def conv_kernel(in_ref, out_ref, filt_ref, toep_ref, pad_ref, flip_ref, back_ref, acc_ref, outer_ref, diag_ref):
    width = 2 * ROWS + 1
    nb = in_ref.shape[0] // width
    half = nb // 2
    rows = half * ROWS
    row = lax.broadcasted_iota(jnp.int32, (B, B), 0)
    lane = lax.broadcasted_iota(jnp.int32, (B, B), 1)
    filt_ref[0:1, :] = jnp.zeros((1, B), F32)
    filt_ref[nb + 1 :, :] = jnp.zeros((7, B), F32)
    filt_ref[pl.ds(1, nb), :] = in_ref[pl.ds(2 * ROWS, nb, stride=width), :]
    for r in range(ROWS):
        for p in range(2):
            take = in_ref[pl.ds(r + p * width, half, stride=2 * width), :]
            pad_ref[p, pl.ds(rows + r, half, stride=ROWS), :] = take
            take = in_ref[pl.ds(ROWS + r + p * width, half, stride=2 * width), :]
            acc_ref[p, pl.ds(r, half, stride=ROWS), :] = take
    pad_ref[:, 0:rows, :] = jnp.zeros((2, rows, B), F32)
    flip = jnp.where(lane + row == B - 1, 1.0, 0.0).astype(BF16)
    flip_ref[:, 0:rows, :] = jnp.zeros((2, rows, B), F32)
    for p in range(2):
        part = pad_ref[p, rows : 2 * rows, :].astype(BF16)
        flip_ref[p, rows : 2 * rows, :] = jnp.dot(part, flip, preferred_element_type=F32)
    back_ref[...] = beside(acc_ref[...]).T.astype(BF16)
    acc_ref[...] = jnp.zeros((2, rows, B), F32)
    outer_ref[0:4] = jnp.zeros((4, B, B), F32)

    toep_ref[(nb + 2) * B :, :] = jnp.zeros((B, B), BF16)

    def build(dist):
        now = jnp.broadcast_to(filt_ref[pl.ds(dist + 1, 1), :], (B, B))
        before = jnp.broadcast_to(filt_ref[pl.ds(dist, 1), :], (B, B))
        block = pltpu.roll(jnp.where(lane + row < B, now, before), 0, 1, stride=1, stride_axis=0)
        at = pl.multiple_of((nb + 1 - dist) * B, B)
        toep_ref[pl.ds(at, B), :] = block.astype(BF16)

    def diagonal(at):
        picked = jnp.where(lane + row >= B - 1, outer_ref[at], outer_ref[at + 1])
        rolled = pltpu.roll(picked, 0, 1, stride=1, stride_axis=0)
        diag_ref[pl.ds(at, 1), :] = jnp.sum(rolled, axis=0, keepdims=True)

    def step(d, live, deep):
        even = pl.multiple_of((nb + 1 - 2 * d) * B, B)
        odd = pl.multiple_of((nb - 2 * d) * B, B)
        taps = jnp.concatenate([toep_ref[pl.ds(even, 2 * B), :], toep_ref[pl.ds(odd, 2 * B), :]], axis=1)
        start = pl.multiple_of(2 * rows - live - ROWS * d, ROWS)
        shifted = beside(pad_ref[:, pl.ds(start, live), :]).astype(BF16)
        ahead = jnp.dot(shifted, taps, preferred_element_type=F32)
        start = pl.multiple_of(2 * rows - deep - ROWS * d, ROWS)
        flipped = beside(flip_ref[:, pl.ds(start, deep), :]).astype(BF16)
        outer = jnp.dot(back_ref[:, rows - deep :], flipped, preferred_element_type=F32)
        build(2 * d + 2)
        build(2 * d + 3)
        diagonal(2 * d)
        diagonal(2 * d + 1)
        acc_ref[0, rows - live :, :] += ahead[:, 0:B]
        acc_ref[1, rows - live :, :] += ahead[:, B : 2 * B]
        outer_ref[2 * d + 3] += outer[0:B, B : 2 * B]
        outer_ref[2 * d + 4] = outer[0:B, 0:B] + outer[B : 2 * B, B : 2 * B]
        outer_ref[2 * d + 5] = outer[B : 2 * B, 0:B]

    build(0)
    build(1)
    phases = 4
    for phase in range(phases):
        live = rows * (phases - phase) // phases
        deep = min(rows, -(-live // B) * B)

        def some(d, _, live=live, deep=deep):
            step(d, live, deep)
            return 0

        lax.fori_loop(half * phase // phases, half * (phase + 1) // phases, some, 0, unroll=8)
    outer_ref[nb + 4] = jnp.zeros((B, B), F32)
    for at in range(nb, nb + 4):
        diagonal(at)
    for r in range(ROWS):
        for p in range(2):
            at = pl.ds(r + p * (ROWS + 1), half, stride=2 * (ROWS + 1))
            out_ref[at, :] = acc_ref[p, pl.ds(r, half, stride=ROWS), :]
    out_ref[pl.ds(ROWS, nb, stride=ROWS + 1), :] = pltpu.roll(diag_ref[pl.ds(4, nb), :], 1, 1)


def convolve(x):
    nb = x.shape[0] // (2 * ROWS + 1)
    half = nb // 2
    return pl.pallas_call(
        conv_kernel,
        out_shape=jax.ShapeDtypeStruct((nb * (ROWS + 1), B), F32),
        in_specs=[VMEM],
        out_specs=VMEM,
        scratch_shapes=[
            pltpu.VMEM((nb + 8, B), F32),
            pltpu.VMEM(((nb + 3) * B, B), BF16),
            pltpu.VMEM((2, 2 * half * ROWS, B), F32),
            pltpu.VMEM((2, 2 * half * ROWS, B), F32),
            pltpu.VMEM((2 * B, half * ROWS), BF16),
            pltpu.VMEM((2, half * ROWS, B), F32),
            pltpu.VMEM((nb + 6, B, B), F32),
            pltpu.VMEM((nb + 8, B), F32),
        ],
        compiler_params=params(16),
        name="conv",
    )(x)


def fetch(core_ref, w_hbm, w_ref, sem, first):
    blocks, _, wide_n = w_ref.shape

    def copy(i):
        at = pl.multiple_of((2 * (first + i) + core_ref[0]) * wide_n, wide_n)
        return pltpu.make_async_copy(w_hbm.at[:, pl.ds(at, wide_n)], w_ref.at[i], sem.at[i])

    for i in range(blocks):
        copy(i).start()
    return lambda i: copy(i).wait()


def fetch_kernel(core_ref, after_ref, w_hbm, out_ref, sem):
    wait = fetch(core_ref, w_hbm, out_ref, sem, 0)
    for i in range(out_ref.shape[0]):
        wait(i)


def multiply(mixed_ref, w_ref, out_ref, first):
    for i in range(w_ref.shape[0]):
        out_ref[first + i] = jnp.dot(mixed_ref[...], w_ref[i], preferred_element_type=F32)


def first_kernel(core_ref, q_ref, c_ref, ahead_ref, w_hbm, out_ref, mixed_ref, df_ref, turn_ref, w_ref, w_sem):
    width = ROWS + 1
    n = c_ref.shape[0] // width
    nfilt = df_ref.shape[0]
    early = ahead_ref.shape[0]
    wait = fetch(core_ref, w_hbm, w_ref, w_sem, early)
    for r in range(ROWS):
        turn_ref[pl.ds(r, n, stride=ROWS), :] = c_ref[pl.ds(r, n, stride=width), :]
    mixed_ref[...] = (q_ref[...] * turn_ref[...].T).astype(BF16)
    share = n // nfilt
    total = c_ref[pl.ds(ROWS, nfilt, stride=share * width), :]
    for r in range(1, share):
        total += c_ref[pl.ds(r * width + ROWS, nfilt, stride=share * width), :]
    df_ref[...] = total
    multiply(mixed_ref, ahead_ref, out_ref, 0)
    for i in range(w_ref.shape[0]):
        wait(i)
    multiply(mixed_ref, w_ref, out_ref, early)


def second_kernel(core_ref, mixed_ref, w_hbm, out_ref, w_ref, w_sem):
    wait = fetch(core_ref, w_hbm, w_ref, w_sem, 0)
    half = w_ref.shape[0] // 2
    for start in (0, half):
        for i in range(half):
            wait(start + i)
        multiply(mixed_ref, w_ref.at[start : start + half], out_ref, start)


def prefetch(after, w, core, n):
    shape = (n // 4, w.shape[0], w.shape[1] // n)
    return pl.pallas_call(
        fetch_kernel,
        out_shape=jax.ShapeDtypeStruct(shape, BF16),
        in_specs=[SMEM, pl.BlockSpec(memory_space=pl.ANY), HBM],
        out_specs=VMEM,
        scratch_shapes=[pltpu.SemaphoreType.DMA(shape[:1])],
        cost_estimate=pl.CostEstimate(flops=0, bytes_accessed=w.size, transcendentals=0),
        compiler_params=params(46),
        name="prefetch",
    )((1 - core).reshape(1), after, w)


def project(q, c, w, w_theirs, core, nfilt):
    slab, chans = q.shape
    early, _, wide_n = w_theirs.shape
    pairs = w.shape[1] // wide_n // 2
    cost = pl.CostEstimate(flops=slab * chans * w.shape[1], bytes_accessed=w.size, transcendentals=0)
    out = jax.ShapeDtypeStruct((pairs, slab, wide_n), F32)
    mix = jax.ShapeDtypeStruct((slab, chans), BF16)
    df = jax.ShapeDtypeStruct((nfilt, B), F32)
    theirs, mixed, df = pl.pallas_call(
        first_kernel,
        out_shape=(out, mix, df),
        in_specs=[SMEM, VMEM, VMEM, VMEM, HBM],
        out_specs=(VMEM, VMEM, VMEM),
        scratch_shapes=[
            pltpu.VMEM((chans, B), F32),
            pltpu.VMEM((pairs - early, chans, wide_n), BF16),
            pltpu.SemaphoreType.DMA((pairs - early,)),
        ],
        cost_estimate=cost,
        compiler_params=params(46),
        name="theirs",
    )((1 - core).reshape(1), q, c, w_theirs, w)
    mine = pl.pallas_call(
        second_kernel,
        out_shape=out,
        in_specs=[SMEM, VMEM, HBM],
        out_specs=VMEM,
        scratch_shapes=[pltpu.VMEM((pairs, chans, wide_n), BF16), pltpu.SemaphoreType.DMA((pairs,))],
        cost_estimate=cost,
        compiler_params=params(46),
        name="mine",
    )(core.reshape(1), mixed, w)
    return theirs, mine, df


def on_device(query, keys, values, filters, w_out, grad_z):
    parts = lax.axis_size(CONTEXT)
    n = lax.axis_size(TENSOR)
    nfilt = filters.shape[1]
    core = lax.axis_index("core").astype(jnp.int32)

    def exchange(x):
        x = x.reshape(parts, 1, -1)
        return lax.all_to_all(x, CONTEXT, split_axis=0, concat_axis=0, tiled=True).reshape(-1, B)

    whole = exchange(gate(query, keys, values, filters, grad_z, parts, 1 - core))
    result = convolve(whole)
    w_theirs = prefetch(result, w_out, core, n)
    back = exchange(result)
    theirs, mine, grad_filters = project(query, back, w_out, w_theirs, core, nfilt)
    swapped = lax.ppermute(theirs, "core", [(0, 1), (1, 0)])
    summed = mine + swapped
    pieces = lax.all_to_all(summed, ("y", "xh"), split_axis=0, concat_axis=0, tiled=True)
    return jnp.sum(pieces, axis=0), grad_filters.T


def solution(mesh):
    fine = Mesh(
        np.asarray(mesh.devices).reshape([size for _, size in FINE]),
        [name for name, _ in FINE],
    )
    both = P(CONTEXT, TENSOR)
    return jax.shard_map(
        on_device,
        mesh=fine,
        in_specs=(both, both, both, both, P(TENSOR, None), both),
        out_specs=(both, both),
        check_vma=False,
    )
```

```python
import jax
import jax.numpy as jnp
import numpy as np
from jax import lax
from jax.experimental import pallas as pl
from jax.experimental.pallas import tpu as pltpu
from jax.sharding import Mesh, PartitionSpec as P

FINE = (("y", 4), ("xh", 2), ("core", 2), ("xl", 2), ("z", 32))
TENSOR = ("y", "xh", "core")
CONTEXT = ("xl", "z")
ROWS = 8
B = 128
F32 = jnp.float32
BF16 = jnp.bfloat16
VMEM = pl.BlockSpec(memory_space=pltpu.VMEM)
HBM = pl.BlockSpec(memory_space=pltpu.HBM)
SMEM = pl.BlockSpec(memory_space=pltpu.SMEM)
LATER_NS = 24000


def params(mib):
    return pltpu.CompilerParams(vmem_limit_bytes=mib << 20)


def gate_kernel(wait_ref, q_hbm, k_hbm, v_hbm, z_hbm, f_hbm, out_ref, in_ref, f_ref, turn_ref, sem):
    width = 2 * ROWS + 1
    n = out_ref.shape[0] // width
    share = n // f_ref.shape[0]
    copies = [pltpu.make_async_copy(f_hbm, f_ref, sem.at[4])]
    for i, hbm in enumerate((k_hbm, v_hbm, z_hbm, q_hbm)):
        copies.append(pltpu.make_async_copy(hbm, in_ref.at[i], sem.at[i]))
    for copy in copies:
        copy.start()
    copies[0].wait()
    for r in range(share):
        out_ref[pl.ds(r * width + 2 * ROWS, n // share, stride=share * width), :] = f_ref[...]
    for i in range(2):
        copies[2 * i + 1].wait()
        copies[2 * i + 2].wait()
        turn_ref[i] = (in_ref[2 * i] * in_ref[2 * i + 1]).T
        for r in range(ROWS):
            rows = turn_ref[i, pl.ds(r, n, stride=ROWS), :]
            out_ref[pl.ds(i * ROWS + r, n, stride=width), :] = rows

    @pl.when(wait_ref[0] == 1)
    def _():
        pl.delay(LATER_NS)


def gate(q, k, v, f, z, parts, later):
    return pl.pallas_call(
        gate_kernel,
        out_shape=jax.ShapeDtypeStruct((parts * (2 * ROWS + 1), B), F32),
        in_specs=[SMEM] + [HBM] * 5,
        out_specs=VMEM,
        scratch_shapes=[
            pltpu.VMEM((4,) + q.shape, F32),
            pltpu.VMEM(f.shape[::-1], F32),
            pltpu.VMEM((2, q.shape[1], B), F32),
            pltpu.SemaphoreType.DMA((5,)),
        ],
        compiler_params=params(60),
        name="gate",
    )(later.reshape(1), q, k, v, z, f.T)


def beside(x):
    return jnp.concatenate([x[0], x[1]], axis=-1)


def conv_kernel(in_ref, out_ref, filt_ref, toep_ref, pad_ref, flip_ref, back_ref, acc_ref, outer_ref, diag_ref):
    width = 2 * ROWS + 1
    nb = in_ref.shape[0] // width
    half = nb // 2
    rows = half * ROWS
    row = lax.broadcasted_iota(jnp.int32, (B, B), 0)
    lane = lax.broadcasted_iota(jnp.int32, (B, B), 1)
    filt_ref[0:1, :] = jnp.zeros((1, B), F32)
    filt_ref[nb + 1 :, :] = jnp.zeros((7, B), F32)
    filt_ref[pl.ds(1, nb), :] = in_ref[pl.ds(2 * ROWS, nb, stride=width), :]
    for r in range(ROWS):
        for p in range(2):
            take = in_ref[pl.ds(r + p * width, half, stride=2 * width), :]
            pad_ref[p, pl.ds(rows + r, half, stride=ROWS), :] = take
            take = in_ref[pl.ds(ROWS + r + p * width, half, stride=2 * width), :]
            acc_ref[p, pl.ds(r, half, stride=ROWS), :] = take
    pad_ref[:, 0:rows, :] = jnp.zeros((2, rows, B), F32)
    flip = jnp.where(lane + row == B - 1, 1.0, 0.0).astype(BF16)
    flip_ref[:, 0:rows, :] = jnp.zeros((2, rows, B), F32)
    for p in range(2):
        part = pad_ref[p, rows : 2 * rows, :].astype(BF16)
        flip_ref[p, rows : 2 * rows, :] = jnp.dot(part, flip, preferred_element_type=F32)
    back_ref[...] = beside(acc_ref[...]).T.astype(BF16)
    acc_ref[...] = jnp.zeros((2, rows, B), F32)
    outer_ref[0:4] = jnp.zeros((4, B, B), F32)

    toep_ref[(nb + 2) * B :, :] = jnp.zeros((B, B), BF16)

    def build(dist):
        now = jnp.broadcast_to(filt_ref[pl.ds(dist + 1, 1), :], (B, B))
        before = jnp.broadcast_to(filt_ref[pl.ds(dist, 1), :], (B, B))
        block = pltpu.roll(jnp.where(lane + row < B, now, before), 0, 1, stride=1, stride_axis=0)
        at = pl.multiple_of((nb + 1 - dist) * B, B)
        toep_ref[pl.ds(at, B), :] = block.astype(BF16)

    def diagonal(at):
        picked = jnp.where(lane + row >= B - 1, outer_ref[at], outer_ref[at + 1])
        rolled = pltpu.roll(picked, 0, 1, stride=1, stride_axis=0)
        diag_ref[pl.ds(at, 1), :] = jnp.sum(rolled, axis=0, keepdims=True)

    def step(d, live, deep):
        even = pl.multiple_of((nb + 1 - 2 * d) * B, B)
        odd = pl.multiple_of((nb - 2 * d) * B, B)
        taps = jnp.concatenate([toep_ref[pl.ds(even, 2 * B), :], toep_ref[pl.ds(odd, 2 * B), :]], axis=1)
        start = pl.multiple_of(2 * rows - live - ROWS * d, ROWS)
        shifted = beside(pad_ref[:, pl.ds(start, live), :]).astype(BF16)
        ahead = jnp.dot(shifted, taps, preferred_element_type=F32)
        start = pl.multiple_of(2 * rows - deep - ROWS * d, ROWS)
        flipped = beside(flip_ref[:, pl.ds(start, deep), :]).astype(BF16)
        outer = jnp.dot(back_ref[:, rows - deep :], flipped, preferred_element_type=F32)
        build(2 * d + 2)
        build(2 * d + 3)
        diagonal(2 * d)
        diagonal(2 * d + 1)
        acc_ref[0, rows - live :, :] += ahead[:, 0:B]
        acc_ref[1, rows - live :, :] += ahead[:, B : 2 * B]
        outer_ref[2 * d + 3] += outer[0:B, B : 2 * B]
        outer_ref[2 * d + 4] = outer[0:B, 0:B] + outer[B : 2 * B, B : 2 * B]
        outer_ref[2 * d + 5] = outer[B : 2 * B, 0:B]

    build(0)
    build(1)
    phases = 4
    for phase in range(phases):
        live = rows * (phases - phase) // phases
        deep = min(rows, -(-live // B) * B)

        def some(d, _, live=live, deep=deep):
            step(d, live, deep)
            return 0

        lax.fori_loop(half * phase // phases, half * (phase + 1) // phases, some, 0, unroll=8)
    outer_ref[nb + 4] = jnp.zeros((B, B), F32)
    for at in range(nb, nb + 4):
        diagonal(at)
    for r in range(ROWS):
        for p in range(2):
            at = pl.ds(r + p * (ROWS + 1), half, stride=2 * (ROWS + 1))
            out_ref[at, :] = acc_ref[p, pl.ds(r, half, stride=ROWS), :]
    out_ref[pl.ds(ROWS, nb, stride=ROWS + 1), :] = pltpu.roll(diag_ref[pl.ds(4, nb), :], 1, 1)


def convolve(x):
    nb = x.shape[0] // (2 * ROWS + 1)
    half = nb // 2
    return pl.pallas_call(
        conv_kernel,
        out_shape=jax.ShapeDtypeStruct((nb * (ROWS + 1), B), F32),
        in_specs=[VMEM],
        out_specs=VMEM,
        scratch_shapes=[
            pltpu.VMEM((nb + 8, B), F32),
            pltpu.VMEM(((nb + 3) * B, B), BF16),
            pltpu.VMEM((2, 2 * half * ROWS, B), F32),
            pltpu.VMEM((2, 2 * half * ROWS, B), F32),
            pltpu.VMEM((2 * B, half * ROWS), BF16),
            pltpu.VMEM((2, half * ROWS, B), F32),
            pltpu.VMEM((nb + 6, B, B), F32),
            pltpu.VMEM((nb + 8, B), F32),
        ],
        compiler_params=params(16),
        name="conv",
    )(x)


def fetch(core_ref, w_hbm, w_ref, sem, first):
    blocks, _, wide_n = w_ref.shape

    def copy(i):
        at = pl.multiple_of((2 * (first + i) + core_ref[0]) * wide_n, wide_n)
        return pltpu.make_async_copy(w_hbm.at[:, pl.ds(at, wide_n)], w_ref.at[i], sem.at[i])

    for i in range(blocks):
        copy(i).start()
    return lambda i: copy(i).wait()


def fetch_kernel(core_ref, after_ref, w_hbm, out_ref, sem):
    wait = fetch(core_ref, w_hbm, out_ref, sem, 0)
    for i in range(out_ref.shape[0]):
        wait(i)


def multiply(mixed_ref, w_ref, out_ref, first):
    for i in range(w_ref.shape[0]):
        out_ref[first + i] = jnp.dot(mixed_ref[...], w_ref[i], preferred_element_type=F32)


def first_kernel(core_ref, q_ref, c_ref, ahead_ref, w_hbm, out_ref, mixed_ref, df_ref, turn_ref, w_ref, w_sem):
    width = ROWS + 1
    n = c_ref.shape[0] // width
    nfilt = df_ref.shape[0]
    early = ahead_ref.shape[0]
    wait = fetch(core_ref, w_hbm, w_ref, w_sem, early)
    for r in range(ROWS):
        turn_ref[pl.ds(r, n, stride=ROWS), :] = c_ref[pl.ds(r, n, stride=width), :]
    mixed_ref[...] = (q_ref[...] * turn_ref[...].T).astype(BF16)
    share = n // nfilt
    total = c_ref[pl.ds(ROWS, nfilt, stride=share * width), :]
    for r in range(1, share):
        total += c_ref[pl.ds(r * width + ROWS, nfilt, stride=share * width), :]
    df_ref[...] = total
    multiply(mixed_ref, ahead_ref, out_ref, 0)
    for i in range(w_ref.shape[0]):
        wait(i)
    multiply(mixed_ref, w_ref, out_ref, early)


def second_kernel(core_ref, mixed_ref, w_hbm, out_ref, w_ref, w_sem):
    wait = fetch(core_ref, w_hbm, w_ref, w_sem, 0)
    half = w_ref.shape[0] // 2
    for start in (0, half):
        for i in range(half):
            wait(start + i)
        multiply(mixed_ref, w_ref.at[start : start + half], out_ref, start)


def prefetch(after, w, core, n):
    shape = (n // 4, w.shape[0], w.shape[1] // n)
    return pl.pallas_call(
        fetch_kernel,
        out_shape=jax.ShapeDtypeStruct(shape, BF16),
        in_specs=[SMEM, pl.BlockSpec(memory_space=pl.ANY), HBM],
        out_specs=VMEM,
        scratch_shapes=[pltpu.SemaphoreType.DMA(shape[:1])],
        cost_estimate=pl.CostEstimate(flops=0, bytes_accessed=w.size, transcendentals=0),
        compiler_params=params(46),
        name="prefetch",
    )((1 - core).reshape(1), after, w)


def project(q, c, w, w_theirs, core, nfilt):
    slab, chans = q.shape
    early, _, wide_n = w_theirs.shape
    pairs = w.shape[1] // wide_n // 2
    cost = pl.CostEstimate(flops=slab * chans * w.shape[1], bytes_accessed=w.size, transcendentals=0)
    out = jax.ShapeDtypeStruct((pairs, slab, wide_n), F32)
    mix = jax.ShapeDtypeStruct((slab, chans), BF16)
    df = jax.ShapeDtypeStruct((nfilt, B), F32)
    theirs, mixed, df = pl.pallas_call(
        first_kernel,
        out_shape=(out, mix, df),
        in_specs=[SMEM, VMEM, VMEM, VMEM, HBM],
        out_specs=(VMEM, VMEM, VMEM),
        scratch_shapes=[
            pltpu.VMEM((chans, B), F32),
            pltpu.VMEM((pairs - early, chans, wide_n), BF16),
            pltpu.SemaphoreType.DMA((pairs - early,)),
        ],
        cost_estimate=cost,
        compiler_params=params(46),
        name="theirs",
    )((1 - core).reshape(1), q, c, w_theirs, w)
    mine = pl.pallas_call(
        second_kernel,
        out_shape=out,
        in_specs=[SMEM, VMEM, HBM],
        out_specs=VMEM,
        scratch_shapes=[pltpu.VMEM((pairs, chans, wide_n), BF16), pltpu.SemaphoreType.DMA((pairs,))],
        cost_estimate=cost,
        compiler_params=params(46),
        name="mine",
    )(core.reshape(1), mixed, w)
    return theirs, mine, df


def on_device(query, keys, values, filters, w_out, grad_z):
    parts = lax.axis_size(CONTEXT)
    n = lax.axis_size(TENSOR)
    nfilt = filters.shape[1]
    core = lax.axis_index("core").astype(jnp.int32)

    def exchange(x):
        x = x.reshape(parts, 1, -1)
        return lax.all_to_all(x, CONTEXT, split_axis=0, concat_axis=0, tiled=True).reshape(-1, B)

    whole = exchange(gate(query, keys, values, filters, grad_z, parts, 1 - core))
    result = convolve(whole)
    w_theirs = prefetch(result, w_out, core, n)
    back = exchange(result)
    theirs, mine, grad_filters = project(query, back, w_out, w_theirs, core, nfilt)
    swapped = lax.ppermute(theirs, "core", [(0, 1), (1, 0)])
    summed = mine + swapped
    pieces = lax.all_to_all(summed, ("y", "xh"), split_axis=0, concat_axis=0, tiled=True)
    return jnp.sum(pieces, axis=0), grad_filters.T


def solution(mesh):
    fine = Mesh(
        np.asarray(mesh.devices).reshape([size for _, size in FINE]),
        [name for name, _ in FINE],
    )
    both = P(CONTEXT, TENSOR)
    return jax.shard_map(
        on_device,
        mesh=fine,
        in_specs=(both, both, both, both, P(TENSOR, None), both),
        out_specs=(both, both),
        check_vma=False,
    )
```
